128 devices in a mesh: dp: 16 (over y_hi, z, core), cache: 8 (over y_lo, x).
Axes of the slice: x: 4, y: 4 (y_hi: 2, y_lo: 2; y = y_hi * 2 + y_lo), z: 4, core: 2. Of those that a mesh axis runs over, the one named last changes fastest.
Arguments:
- hidden_in: bfloat16 [16384, 2560], P(('dp', 'cache')), may hold values from -6 to 6
- placing: int32 [16384], P('dp'), may hold values from 0 to 16383, as said below
- prompt_start: int32 [16384], P(('dp', 'cache')), may hold values from 0 to 16383, as said below
- attn_gain: float32 [2560], replicated, may hold values from 0.5 to 1.5
- w_qkv: bfloat16 [2560, 1792], P(('dp', 'cache'))
- w_out: bfloat16 [1280, 2560], P(('dp', 'cache')), may hold values from -0.15625 to 0.15625
- moe_gain: float32 [2560], replicated, may hold values from 0.5 to 1.5
- routes: int32 [16384, 6], P(('dp', 'cache')), may hold values from 0 to 63, all different within a row; in each aligned block of 128 rows (0 to 127, 128 to 255, ...) at most 16 rows name the same one
- route_weight: float32 [16384, 6], P(('dp', 'cache')), may hold values from 0.05 to 0.35
- w_gate_up: bfloat16 [128, 2560, 1536], P(('dp', 'cache')), may hold values from -0.125 to 0.125
- w_down: bfloat16 [128, 768, 2560], P(('dp', 'cache')), may hold values from -0.15625 to 0.15625
Outputs:
- mixed: bfloat16 [16384, 2560], P(('dp', 'cache'))
- cache_keys: bfloat16 [16384, 256], P(('dp', 'cache'))
- cache_values: bfloat16 [16384, 256], P(('dp', 'cache'))
The draws below stay inside these ranges and needn't reach their ends.
Inputs may be any that keep to these rules, and one draw needn't show every extreme that they name: `placing`: a permutation of the 16384 positions; dealt rows g * 1024 to (g+1) * 1024 - 1 hold natural positions of the same range, and the dealt rows c * 128 + j * 16 to c * 128 + (j+1) * 16 - 1 of a group hold natural positions of its span j * 128 to (j+1) * 128 - 1. Prompts are runs of consecutive natural positions inside one group of 1024, of at most 512 tokens, some of exactly 512; prompt_start[r] <= placing[r] and it is the first position of that run. `routes`: in the rows of one device (aligned blocks of 128 rows) no expert is named more than 16 times.
All inputs are finite; a program needn't handle non-finite values.
Results may differ from the reference program's by a relative error of at most 0.014.
Values may be sent and summed in bfloat16 or wider, within the bound.
No kernel may reach another device: no remote copies, remote signals or barrier semaphores. Data moves between devices by JAX's collectives and lax.ppermute only.
A program may use at most 128 MiB of HBM per device.

```python
import math
import jax
import jax.numpy as jnp
import numpy as np
from jax import lax

D = 2560
HD = 128
QH = 10
KVH = 2
FF = 1536
TOP = 6
TOK_DEV = 128
EXPERTS = 64
HALF_FF = 768
QD = 1280
MOST = 16
GROUP = 1024
DEAL = 16
LMAX = 512
TOKENS = 16384


def deal_tables(key):
    group_count = TOKENS // GROUP
    span_count = GROUP // TOK_DEV
    base_key = jax.random.fold_in(key, 11)
    rate_key, long_key, cut_key, perm_key = jax.random.split(base_key, 4)
    spacing = jnp.array([4, 16, 64, 256], jnp.int32)[jax.random.randint(rate_key, (group_count,), 0, 4)]
    raw_draws = jax.random.randint(cut_key, (group_count, GROUP), 0, 1 << 20)
    index_row = jnp.arange(GROUP, dtype=jnp.int32)
    cutting = raw_draws % spacing[:, None] == 0
    cutting = cutting | (index_row[None, :] % LMAX == 0)
    long_group = jax.random.randint(long_key, (), 0, group_count)
    quiet = (jnp.arange(group_count, dtype=jnp.int32)[:, None] == long_group) & (index_row[None, :] < LMAX) & (index_row[None, :] > 0)
    cutting = cutting & jnp.logical_not(quiet)
    beginning = lax.cummax(jnp.where(cutting, index_row[None, :], 0), axis=1)
    start_table = (beginning + jnp.arange(group_count, dtype=jnp.int32)[:, None] * GROUP).reshape(-1)
    perm_keys = jax.random.split(perm_key, group_count * span_count)
    shuffles = jax.vmap(lambda single: jax.random.permutation(single, TOK_DEV))(perm_keys).astype(jnp.int32)
    shuffles = shuffles.reshape(group_count, span_count, span_count, DEAL)
    shuffles = jnp.transpose(shuffles, (0, 2, 1, 3))
    offsets = jnp.arange(group_count, dtype=jnp.int32)[:, None, None, None] * GROUP + jnp.arange(span_count, dtype=jnp.int32)[None, None, :, None] * TOK_DEV
    place_table = (shuffles + offsets).reshape(-1)
    return (place_table, start_table[place_table])


def draw_placing(key, part):
    return deal_tables(key)[0]


def draw_prompt_start(key, part):
    return deal_tables(key)[1]


def draw_w_qkv(key, part):
    columns = QH * HD + 2 * KVH * HD
    base = jax.random.normal(key, (D, columns), jnp.float32) * D ** (-0.5)
    return base.astype(jnp.bfloat16)


def levels(rng, shape, pieces, low, top_value):
    def one(dim, shards_of):
        heights = jax.random.uniform(jax.random.fold_in(jax.random.fold_in(rng, 6), dim), (shards_of,), jnp.float32, low / len(pieces), top_value / len(pieces))
        return jnp.repeat(jnp.exp(heights), shape[dim] // shards_of).reshape((-1,) + (1,) * (len(shape) - dim - 1))

    factor_of = one(*pieces[0])
    for cut in pieces[1:]:
        factor_of = factor_of * one(*cut)
    return factor_of


def deal_out(stream_key, own, number, rows, number_of, top, bound, lean):
    ranking = jax.random.permutation(stream_key, number_of)
    packed, ordinary = portions_of(number_of, rows * top, bound, lean, True), portions_of(number_of, rows * top, bound, lean, False)
    places = jnp.arange(number_of)

    def named(sizes, rotation):
        used = int((sizes > 0).sum())
        fixed = max(1, used // 4)
        passed = fixed + (places - fixed + rotation * (used - fixed)) % max(1, number_of - fixed)
        return jnp.zeros((number_of,), jnp.int32).at[ranking[jnp.where(places < fixed, places, passed)]].set(jnp.asarray(sizes, jnp.int32))

    sizes = jnp.where(number % 4 == 0, named(packed, number // 4), named(ordinary, number - number // 4 - 1))
    mixed = jax.random.permutation(jax.random.fold_in(own, 3), number_of)
    giver, sink = mixed[0:number_of // 2 * 2:2], mixed[1:number_of // 2 * 2:2]
    margin = jnp.minimum(sizes[giver] - 1, bound - sizes[sink]) // 2
    margin = jnp.where((giver == ranking[0]) | (sink == ranking[0]) | (sizes[sink] == 0), 0, jnp.maximum(margin, 0))
    passed = jax.random.randint(jax.random.fold_in(own, 4), (number_of // 2,), 0, 1 << 20) % (margin + 1)
    sizes = sizes.at[giver].add(-passed).at[sink].add(passed)
    items = jnp.searchsorted(jnp.cumsum(sizes), jnp.arange(rows * top), side="right").astype(jnp.int32)
    table = items.reshape(top, rows).T
    table = table[jax.random.permutation(jax.random.fold_in(own, 1), rows)]
    rotation = jax.random.randint(jax.random.fold_in(own, 2), (rows, 1), 0, top)
    return jnp.take_along_axis(table, (jnp.arange(top)[None, :] + rotation) % top, axis=1)


def portions_of(amount, total, reach, slope, full):
    loads = [(1 << 20) // math.isqrt(grade ** slope) + 1 for grade in range(1, amount + 1)]
    largest = reach if full else min(reach, max(-(-total // amount), total * loads[0] // sum(loads)))
    least = 1 if total - largest >= amount - 1 else 0
    holding, surplus = [largest] + [least] * (amount - 1), total - largest - least * (amount - 1)
    while surplus > 0:
        free = [i for i in range(1, amount) if holding[i] < largest] or [i for i in range(1, amount) if holding[i] < reach]
        whole, left = sum([loads[i] for i in free]), surplus
        for i in free:
            more = min(reach - holding[i], max(1, left * loads[i] // whole), surplus)
            holding[i] = holding[i] + more
            surplus = surplus - more
    return np.array(holding)


def noise(rng, extent, scale, most, cuts=(), kind=jnp.bfloat16):
    drawn = jax.random.normal(rng, extent, jnp.float32) * scale
    if len(cuts) > 0:
        drawn = levels(rng, extent, cuts, -0.22, 0.18) * drawn
    return jnp.clip(drawn, min=-most, max=most).astype(kind)


def setup_inputs(seed: int = 0) -> dict:
    streams_of = jax.random.split(jax.random.key(seed), 12)
    hidden_in = noise(streams_of[0], (TOKENS, D), 1.0, 6.0, ((0, 128),))
    placing = draw_placing(jax.random.fold_in(streams_of[11], 71), 0)
    prompt_start = draw_prompt_start(jax.random.fold_in(streams_of[11], 71), 0)
    attn_gain = jnp.clip(1.0 + 0.1 * jax.random.normal(streams_of[3], (D,), jnp.float32), 0.5, 1.5)
    w_qkv = draw_w_qkv(jax.random.fold_in(streams_of[11], 71), 0)
    w_out = noise(streams_of[5], (QD, D), QD ** -0.5, 0.15625, ((0, 128),))
    moe_gain = jnp.clip(1.0 + 0.1 * jax.random.normal(streams_of[6], (D,), jnp.float32), 0.5, 1.5)
    routes_keys = jax.random.split(jax.random.fold_in(streams_of[7], 1), TOKENS // TOK_DEV)
    routes_turns = jax.random.permutation(jax.random.fold_in(streams_of[7], 3), TOKENS // TOK_DEV)
    routes = jax.vmap(lambda own, number: deal_out(jax.random.fold_in(streams_of[7], 2), own, number, TOK_DEV, EXPERTS, TOP, MOST, 2))(routes_keys, routes_turns).reshape((TOKENS, TOP))
    route_weight = jnp.clip(0.05 + 0.29999999 * jax.random.uniform(streams_of[8], (TOKENS, TOP), jnp.float32) ** levels(streams_of[8], (TOKENS, TOP), ((0, 128),), -0.2, 0.2), 0.05, 0.35)
    w_gate_up = noise(streams_of[9], (2 * EXPERTS, D, FF), D ** -0.5, 0.125, ((0, 128),))
    w_down = noise(streams_of[10], (2 * EXPERTS, HALF_FF, D), FF ** -0.5, 0.15625, ((0, 128),))
    return {"hidden_in": hidden_in, "placing": placing, "prompt_start": prompt_start, "attn_gain": attn_gain, "w_qkv": w_qkv, "w_out": w_out, "moe_gain": moe_gain, "routes": routes, "route_weight": route_weight, "w_gate_up": w_gate_up, "w_down": w_down}


norm_eps = 1e-05
rope_base = 500000.0
masked_score = -1e+30

def rms_scaled(features, gain_vector):
    widened = features.astype(jnp.float32)
    factor = lax.rsqrt(lax.optimization_barrier(jnp.mean(widened * widened, axis=-1, keepdims=True)) + norm_eps)
    return (widened * factor * gain_vector).astype(jnp.bfloat16)

def rotated(projected, position, head_count):
    row_count = projected.shape[0]
    grouped = projected.reshape(row_count, head_count, HD)
    half_size = HD // 2
    inverse = rope_base ** (-(jnp.arange(half_size, dtype=jnp.float32) * 2.0 / HD))
    angles = position.astype(jnp.float32)[:, None] * inverse[None, :]
    cosine = jnp.cos(angles)[:, None, :]
    sine_part = jnp.sin(angles)[:, None, :]
    first_half = grouped[..., :half_size]
    second = grouped[..., half_size:]
    turned = jnp.concatenate([first_half * cosine - second * sine_part, second * cosine + first_half * sine_part], axis=-1)
    return turned.reshape(row_count, head_count * HD).astype(jnp.bfloat16)

def expert_half(slot_block, gate_up, down_part):
    flat_rows = slot_block.reshape(-1, slot_block.shape[-1])
    joined = jnp.dot(flat_rows, gate_up, preferred_element_type=jnp.float32)
    half_size = gate_up.shape[1] // 2
    active = (jax.nn.silu(joined[:, :half_size]) * joined[:, half_size:]).astype(jnp.bfloat16)
    return jnp.dot(active, down_part, preferred_element_type=jnp.float32).astype(jnp.bfloat16).reshape(slot_block.shape)

def attention(queries, keys_all, values_all, placing, prompt_start):
    tokens_all = queries.shape[0]
    group_count = tokens_all // GROUP
    group_size = QH // KVH

    def one_group(pieces_in):
        query_part, key_part, value_part, place_part, start_part = pieces_in
        query_heads = query_part.reshape(GROUP, KVH, group_size, HD).astype(jnp.float32)
        key_heads = key_part.reshape(GROUP, KVH, HD).astype(jnp.float32)
        value_heads = value_part.reshape(GROUP, KVH, HD).astype(jnp.float32)
        scores = jnp.einsum('tkgd,rkd->tkgr', query_heads, key_heads, precision=lax.Precision.HIGHEST) * HD ** (-0.5)
        allowed = (place_part[None, :] >= start_part[:, None]) & (place_part[None, :] <= place_part[:, None])
        allowed = allowed[:, None, None, :]
        highest = lax.optimization_barrier(jnp.max(jnp.where(allowed, scores, masked_score), axis=-1, keepdims=True))
        weights = jnp.where(allowed, jnp.exp(scores - highest), 0.0)
        rounded = lax.optimization_barrier(weights.astype(jnp.bfloat16))
        numerator = jnp.einsum('tkgr,rkd->tkgd', rounded.astype(jnp.float32), value_heads, precision=lax.Precision.HIGHEST)
        context = numerator / lax.optimization_barrier(jnp.sum(weights, axis=-1))[..., None]
        return context.reshape(GROUP, QH * HD).astype(jnp.bfloat16)
    stacked = (queries.reshape(group_count, GROUP, QH * HD), keys_all.reshape(group_count, GROUP, KVH * HD), values_all.reshape(group_count, GROUP, KVH * HD), placing.reshape(group_count, GROUP), prompt_start.reshape(group_count, GROUP))
    return lax.map(one_group, stacked).reshape(tokens_all, QH * HD)

def expert_mix(moe_in, routes, route_weight, w_gate_up, w_down):
    tokens_all = moe_in.shape[0]
    width = 2 * EXPERTS * MOST
    expert_ids = routes.reshape(-1)
    pair_count = expert_ids.shape[0]
    one_hot = (expert_ids[:, None] == jnp.arange(EXPERTS, dtype=jnp.int32)[None, :]).astype(jnp.int32)
    slot_rank = lax.optimization_barrier(jnp.sum((jnp.cumsum(one_hot, axis=0) - one_hot) * one_hot, axis=1))
    slot_index = expert_ids * width + slot_rank
    source_row = jnp.full((EXPERTS * width,), tokens_all, jnp.int32).at[slot_index].set(jnp.arange(pair_count, dtype=jnp.int32) // TOP).reshape(EXPERTS, width)
    weight_of = jnp.zeros((EXPERTS * width,), jnp.float32).at[slot_index].set(route_weight.reshape(-1)).reshape(EXPERTS, width)
    padded = jnp.concatenate([moe_in, jnp.zeros((1, moe_in.shape[1]), moe_in.dtype)], axis=0)
    halves_up = w_gate_up.reshape(EXPERTS, 2, w_gate_up.shape[1], w_gate_up.shape[2])
    halves_down = w_down.reshape(EXPERTS, 2, w_down.shape[1], w_down.shape[2])

    def step(running, pieces_in):
        row_index, weight_row, gate_up, down_part = pieces_in
        slot_block = padded[row_index]
        first_part = expert_half(slot_block, gate_up[0], down_part[0]).astype(jnp.float32)
        second_part = expert_half(slot_block, gate_up[1], down_part[1]).astype(jnp.float32)
        output = (first_part + second_part).astype(jnp.bfloat16)
        running = running.at[row_index].add(weight_row[:, None] * output.astype(jnp.float32))
        return (running, None)
    running, _ = lax.scan(step, jnp.zeros((tokens_all + 1, moe_in.shape[1]), jnp.float32), (source_row, weight_of, halves_up, halves_down))
    return running[:tokens_all]

def reference(hidden_in, placing, prompt_start, attn_gain, w_qkv, w_out, moe_gain, routes, route_weight, w_gate_up, w_down):
    query_width = QH * HD
    kv_width = KVH * HD
    normed = rms_scaled(hidden_in, attn_gain)
    projected = jnp.dot(normed, w_qkv, preferred_element_type=jnp.float32)
    position = (placing - prompt_start).astype(jnp.int32)
    queries = rotated(projected[:, :query_width], position, QH)
    keys_here = rotated(projected[:, query_width:query_width + kv_width], position, KVH)
    values_here = projected[:, query_width + kv_width:].astype(jnp.bfloat16)
    context = attention(queries, keys_here, values_here, placing, prompt_start)
    attended = (hidden_in.astype(jnp.float32) + jnp.dot(context, w_out, preferred_element_type=jnp.float32)).astype(jnp.bfloat16)
    moe_in = rms_scaled(attended, moe_gain)
    mixture = expert_mix(moe_in, routes, route_weight, w_gate_up, w_down)
    finished = (attended.astype(jnp.float32) + mixture).astype(jnp.bfloat16)
    mixed = jnp.zeros_like(finished).at[placing].set(finished)
    cache_keys = jnp.zeros_like(keys_here).at[placing].set(keys_here)
    cache_values = jnp.zeros_like(values_here).at[placing].set(values_here)
    return (mixed, cache_keys, cache_values)
```

```python
import jax
import jax.numpy as jnp
import numpy as np
from jax import lax
from jax.sharding import Mesh
from jax.sharding import PartitionSpec as P

HD = 128
QH = 10
KVH = 2
TOP = 6
MOST = 16

DP = ("yh", "z", "core")
CACHE = ("yl", "x")
SIZES = {"yh": 2, "z": 4, "core": 2, "yl": 2, "x": 4}
ALL = DP + CACHE
CHIPS = ("yh", "z", "yl", "x")
CHIP_COUNT = 64

norm_eps = 1e-05
rope_base = 500000.0
masked_score = -1e30


def linear(yh, z, core, yl, x):
    return (((yh * 4 + z) * 2 + core) * 2 + yl) * 4 + x


def swap_pairs():
    pairs = []
    for yh in range(2):
        for z in range(4):
            for yl in range(2):
                for x in range(0, 4, 2):
                    low = linear(yh, z, 1, yl, x)
                    high = linear(yh, z, 0, yl, x + 1)
                    pairs += [(low, high), (high, low)]
    return pairs


def rms_scaled(features, gain_vector):
    widened = features.astype(jnp.float32)
    factor = lax.rsqrt(jnp.mean(widened * widened, axis=-1, keepdims=True) + norm_eps)
    return (widened * factor * gain_vector).astype(jnp.bfloat16)


def rotated(grouped, cosine, sine_part):
    half_size = HD // 2
    first_half = grouped[..., :half_size]
    second = grouped[..., half_size:]
    return jnp.concatenate(
        [first_half * cosine - second * sine_part, second * cosine + first_half * sine_part],
        axis=-1,
    ).astype(jnp.bfloat16)


def spread(shard, axes, count):
    return lax.all_to_all(
        jnp.broadcast_to(shard[None], (count,) + shard.shape), axes, 0, 0, tiled=True
    )


def expert_half(rows, gate_up, down_part):
    joined = jnp.dot(rows, gate_up, preferred_element_type=jnp.float32)
    half_size = gate_up.shape[1] // 2
    active = (jax.nn.silu(joined[:, :half_size]) * joined[:, half_size:]).astype(jnp.bfloat16)
    return jnp.dot(active, down_part, preferred_element_type=jnp.float32).astype(jnp.bfloat16)


def per_device(
    hidden_in,
    placing,
    prompt_start,
    attn_gain,
    w_qkv,
    w_out,
    moe_gain,
    routes,
    route_weight,
    w_gate_up,
    w_down,
):
    row_count, model_width = hidden_in.shape
    query_width = QH * HD
    kv_width = KVH * HD
    my_index = lax.axis_index(CACHE)
    group_rows = placing.shape[0]
    cache_size = group_rows // row_count
    deal_rows = row_count // cache_size
    group_base = lax.axis_index(DP) * group_rows

    pairs = swap_pairs()
    other_up = lax.ppermute(w_gate_up[0], ALL, pairs)
    other_down = lax.ppermute(w_down[0], ALL, pairs)
    keep = lax.axis_index("x") % 2 == lax.axis_index("core")

    qkv_rows = spread(w_qkv, CACHE, cache_size).reshape(-1, w_qkv.shape[1])
    full_qkv = lax.all_gather(qkv_rows, DP, axis=0, tiled=True)
    out_rows = spread(w_out, CACHE, cache_size).reshape(-1, w_out.shape[1])
    full_out = lax.all_gather(out_rows, DP, axis=0, tiled=True)
    full_qkv, other_up = lax.optimization_barrier((full_qkv, other_up))
    full_out, other_down = lax.optimization_barrier((full_out, other_down))

    my_place = lax.dynamic_slice_in_dim(placing, my_index * row_count, row_count)
    position = my_place - prompt_start

    bits = routes
    chip_of = (
        (bits & 0b111000)
        | ((bits & 0b000011) << 1)
        | ((bits & 0b000100) >> 2)
    )
    named = chip_of[:, :, None] == jnp.arange(CHIP_COUNT, dtype=jnp.int32)[None, None, :]
    member = jnp.any(named, axis=1)
    weight_of = jnp.sum(jnp.where(named, route_weight[:, :, None], 0.0), axis=1)
    row_ids = jnp.arange(row_count, dtype=jnp.int32)
    before = (row_ids[:, None] > row_ids[None, :]).astype(jnp.bfloat16)
    rank = jnp.dot(before, member.astype(jnp.bfloat16), preferred_element_type=jnp.float32)
    rank = jnp.where(member, rank.astype(jnp.int32), -1).T
    chosen = rank[:, None, :] == jnp.arange(MOST, dtype=jnp.int32)[None, :, None]
    chosen = chosen.reshape(CHIP_COUNT * MOST, row_count)
    pick = chosen.astype(jnp.bfloat16)
    weighted = jnp.where(
        chosen.reshape(CHIP_COUNT, MOST, row_count), weight_of.T[:, None, :], 0.0
    ).reshape(CHIP_COUNT * MOST, row_count)
    weighted_hi = lax.reduce_precision(weighted, 8, 7)
    weighted_lo = (weighted - weighted_hi).astype(jnp.bfloat16)
    blend = jnp.concatenate([weighted_hi.astype(jnp.bfloat16), weighted_lo], axis=1)

    normed = rms_scaled(hidden_in, attn_gain)
    projected = jnp.dot(normed, full_qkv, preferred_element_type=jnp.float32)
    half_size = HD // 2
    inverse = rope_base ** (-(jnp.arange(half_size, dtype=jnp.float32) * 2.0 / HD))
    angles = position.astype(jnp.float32)[:, None] * inverse[None, :]
    cosine = jnp.cos(angles)
    sine_part = jnp.sin(angles)
    keys_here = [
        rotated(projected[:, query_width + k * HD : query_width + (k + 1) * HD], cosine, sine_part)
        for k in range(KVH)
    ]
    values_here = projected[:, query_width + kv_width :].astype(jnp.bfloat16)
    kv_here = jnp.concatenate(keys_here + [values_here], axis=1)
    kv_group = spread(kv_here, CACHE, cache_size).reshape(group_rows, 2 * kv_width)
    queries = jnp.stack(
        [rotated(projected[:, h * HD : (h + 1) * HD], cosine, sine_part) for h in range(QH)]
    )
    allowed = (placing[None, :] >= prompt_start[:, None]) & (placing[None, :] <= my_place[:, None])
    contexts = []
    share = QH // KVH
    for k in range(KVH):
        key_head = kv_group[:, k * HD : (k + 1) * HD]
        value_head = kv_group[:, kv_width + k * HD : kv_width + (k + 1) * HD]
        scores = jnp.einsum(
            "htd,rd->htr",
            queries[k * share : (k + 1) * share],
            key_head,
            preferred_element_type=jnp.float32,
        ) * (HD ** (-0.5))
        scores = jnp.where(allowed[None], scores, masked_score)
        highest = jnp.max(scores, axis=-1, keepdims=True)
        weights = jnp.where(allowed[None], jnp.exp(scores - highest), 0.0)
        denominator = jnp.sum(weights, axis=-1, keepdims=True)
        numerator = jnp.einsum(
            "htr,rd->htd",
            weights.astype(jnp.bfloat16),
            value_head,
            preferred_element_type=jnp.float32,
        )
        contexts.append((numerator / denominator).astype(jnp.bfloat16))
    context = jnp.concatenate(contexts, axis=0)
    context = jnp.concatenate([context[h] for h in range(QH)], axis=1)
    attn_out = jnp.dot(context, full_out, preferred_element_type=jnp.float32)
    attended = (hidden_in.astype(jnp.float32) + attn_out).astype(jnp.bfloat16)
    moe_in = rms_scaled(attended, moe_gain)

    outgoing = jnp.dot(pick, moe_in, preferred_element_type=jnp.float32).astype(jnp.bfloat16)
    mine = lax.all_to_all(
        outgoing.reshape(CHIP_COUNT, MOST, model_width), CHIPS, 0, 0, tiled=True
    ).reshape(CHIP_COUNT * MOST, model_width)
    cores = [(0, 1), (1, 0)]
    mates = lax.ppermute(mine, "core", cores)
    gate_up = jnp.where(keep, w_gate_up[0], other_up)
    down_part = jnp.where(keep, w_down[0], other_down)
    for_mate = expert_half(mates, gate_up, down_part)
    from_mate = lax.ppermute(for_mate, "core", cores)
    own_part = expert_half(mine, gate_up, down_part)
    expert_out = (own_part.astype(jnp.float32) + from_mate.astype(jnp.float32)).astype(jnp.bfloat16)
    returned = lax.all_to_all(
        expert_out.reshape(CHIP_COUNT, MOST, model_width), CHIPS, 0, 0, tiled=True
    ).reshape(CHIP_COUNT * MOST, model_width)
    blended = lax.dot_general(
        blend, returned, (((0,), (0,)), ((), ())), preferred_element_type=jnp.float32
    )
    mixture = blended[:row_count] + blended[row_count:]
    finished = (attended.astype(jnp.float32) + mixture).astype(jnp.bfloat16)

    home_rows = lax.all_to_all(
        finished.reshape(cache_size, deal_rows, model_width), CACHE, 0, 0, tiled=True
    ).reshape(row_count, model_width)
    my_base = group_base + my_index * row_count
    sender_place = lax.dynamic_slice_in_dim(
        placing.reshape(cache_size, row_count), my_index * deal_rows, deal_rows, axis=1
    ).reshape(-1)
    to_row = (sender_place[None, :] - my_base == row_ids[:, None]).astype(jnp.bfloat16)
    mixed = jnp.dot(to_row, home_rows, preferred_element_type=jnp.float32).astype(jnp.bfloat16)
    from_group = (placing[None, :] - my_base == row_ids[:, None]).astype(jnp.bfloat16)
    cached = jnp.dot(from_group, kv_group, preferred_element_type=jnp.float32).astype(jnp.bfloat16)
    return (mixed, cached[:, :kv_width], cached[:, kv_width:])


def solution(mesh):
    fine = Mesh(np.asarray(mesh.devices).reshape(tuple(SIZES[a] for a in ALL)), ALL)
    in_specs = (
        P(ALL, None),
        P(DP),
        P(ALL),
        P(),
        P(ALL, None),
        P(ALL, None),
        P(),
        P(ALL, None),
        P(ALL, None),
        P(ALL, None, None),
        P(ALL, None, None),
    )
    out_specs = (P(ALL, None), P(ALL, None), P(ALL, None))
    return jax.shard_map(
        per_device, mesh=fine, in_specs=in_specs, out_specs=out_specs, check_vma=False
    )
```

```python
import jax
import jax.numpy as jnp
import numpy as np
from jax import lax
from jax.sharding import Mesh
from jax.sharding import PartitionSpec as P

HD = 128
QH = 10
KVH = 2
TOP = 6
MOST = 16

DP = ("yh", "z", "core")
CACHE = ("yl", "x")
SIZES = {"yh": 2, "z": 4, "core": 2, "yl": 2, "x": 4}
ALL = DP + CACHE
CHIPS = ("yh", "z", "yl", "x")
CHIP_COUNT = 64

norm_eps = 1e-05
rope_base = 500000.0
masked_score = -1e30


def linear(yh, z, core, yl, x):
    return (((yh * 4 + z) * 2 + core) * 2 + yl) * 4 + x


def swap_pairs():
    pairs = []
    for yh in range(2):
        for z in range(4):
            for yl in range(2):
                for x in range(0, 4, 2):
                    low = linear(yh, z, 1, yl, x)
                    high = linear(yh, z, 0, yl, x + 1)
                    pairs += [(low, high), (high, low)]
    return pairs


def rms_scaled(features, gain_vector):
    widened = features.astype(jnp.float32)
    factor = lax.rsqrt(jnp.mean(widened * widened, axis=-1, keepdims=True) + norm_eps)
    return (widened * factor * gain_vector).astype(jnp.bfloat16)


def rotated(grouped, cosine, sine_part):
    half_size = HD // 2
    first_half = grouped[..., :half_size]
    second = grouped[..., half_size:]
    return jnp.concatenate(
        [first_half * cosine - second * sine_part, second * cosine + first_half * sine_part],
        axis=-1,
    ).astype(jnp.bfloat16)


def spread(shard, axes, count):
    return lax.all_to_all(
        jnp.broadcast_to(shard[None], (count,) + shard.shape), axes, 0, 0, tiled=True
    )


def ring(block, axes):
    half = block.shape[0] // 2
    upward = [(i, (i + 1) % 4) for i in range(4)]
    downward = [(i, (i - 1) % 4) for i in range(4)]
    below = lax.ppermute(block, axes, upward)
    above = lax.ppermute(block, axes, downward)
    far_low = lax.ppermute(below[:half], axes, upward)
    far_high = lax.ppermute(above[half:], axes, downward)
    return jnp.concatenate([block, below, above, far_low, far_high], axis=0)


RING_Y = ("yh", "yl")
STEPS = (0, -1, 1, 2)
CORES = [(0, 1), (1, 0)]


def source_features(block_rows, y_outer, flip):
    count = 16 * block_rows
    index = jnp.arange(count, dtype=jnp.int32)
    offsets = jnp.array(STEPS, jnp.int32)
    outer = offsets[index // (4 * block_rows)]
    inner = offsets[index // block_rows % 4]
    dy, dz = (outer, inner) if y_outer else (inner, outer)
    y = (lax.axis_index(RING_Y) + dy) % 4
    z = (lax.axis_index("z") + dz) % 4
    core = lax.axis_index("core")
    core = 1 - core if flip else core
    block = (((y // 2) * 4 + z) * 2 + core) * 2 + y % 2
    return block * block_rows + index % block_rows


def reordered(features, order):
    count = features.shape[1]
    ids = jnp.arange(count, dtype=jnp.int32)
    take = (ids[:, None] == order[None, :]).astype(jnp.bfloat16)
    return jnp.dot(features, take, preferred_element_type=jnp.float32).astype(jnp.bfloat16)


def expert_half(rows, gate_up, down_part):
    joined = jnp.dot(rows, gate_up, preferred_element_type=jnp.float32)
    half_size = gate_up.shape[1] // 2
    active = (jax.nn.silu(joined[:, :half_size]) * joined[:, half_size:]).astype(jnp.bfloat16)
    return jnp.dot(active, down_part, preferred_element_type=jnp.float32).astype(jnp.bfloat16)


def per_device(
    hidden_in,
    placing,
    prompt_start,
    attn_gain,
    w_qkv,
    w_out,
    moe_gain,
    routes,
    route_weight,
    w_gate_up,
    w_down,
):
    row_count, model_width = hidden_in.shape
    query_width = QH * HD
    kv_width = KVH * HD
    my_index = lax.axis_index(CACHE)
    group_rows = placing.shape[0]
    cache_size = group_rows // row_count
    deal_rows = row_count // cache_size
    group_base = lax.axis_index(DP) * group_rows

    pairs = swap_pairs()
    up_rows = w_gate_up.shape[1] // 2
    other_low = lax.ppermute(w_gate_up[0, :up_rows], ALL, pairs)
    other_high = lax.ppermute(w_gate_up[0, up_rows:], ALL, pairs)
    other_down = lax.ppermute(w_down[0], ALL, pairs)
    keep = lax.axis_index("x") % 2 == lax.axis_index("core")

    block = spread(w_qkv, "x", 4).reshape(-1, w_qkv.shape[1])
    block_rows = block.shape[0]
    half_width = block.shape[1] // 2
    first = ring(ring(block[:, :half_width], "z"), RING_Y)
    last = ring(ring(block[:, half_width:], RING_Y), "z")
    last_other = lax.ppermute(last, "core", CORES)
    first_other = lax.ppermute(first, "core", CORES)
    out_rows = spread(w_out, CACHE, cache_size).reshape(-1, w_out.shape[1])
    full_out = lax.all_gather(out_rows, DP, axis=0, tiled=True)
    last_other, other_low = lax.optimization_barrier((last_other, other_low))
    full_out, other_high = lax.optimization_barrier((full_out, other_high))

    my_place = lax.dynamic_slice_in_dim(placing, my_index * row_count, row_count)
    position = my_place - prompt_start

    bits = routes
    chip_of = (
        (bits & 0b111000)
        | ((bits & 0b000011) << 1)
        | ((bits & 0b000100) >> 2)
    )
    named = chip_of[:, :, None] == jnp.arange(CHIP_COUNT, dtype=jnp.int32)[None, None, :]
    member = jnp.any(named, axis=1)
    weight_of = jnp.sum(jnp.where(named, route_weight[:, :, None], 0.0), axis=1)
    row_ids = jnp.arange(row_count, dtype=jnp.int32)
    before = (row_ids[:, None] > row_ids[None, :]).astype(jnp.bfloat16)
    rank = jnp.dot(before, member.astype(jnp.bfloat16), preferred_element_type=jnp.float32)
    rank = jnp.where(member, rank.astype(jnp.int32), -1).T
    chosen = rank[:, None, :] == jnp.arange(MOST, dtype=jnp.int32)[None, :, None]
    chosen = chosen.reshape(CHIP_COUNT * MOST, row_count)
    pick = chosen.astype(jnp.bfloat16)
    weighted = jnp.where(
        chosen.reshape(CHIP_COUNT, MOST, row_count), weight_of.T[:, None, :], 0.0
    ).reshape(CHIP_COUNT * MOST, row_count)
    weighted_hi = lax.reduce_precision(weighted, 8, 7)
    weighted_lo = (weighted - weighted_hi).astype(jnp.bfloat16)
    blend = jnp.concatenate([weighted_hi.astype(jnp.bfloat16), weighted_lo], axis=1)

    normed = rms_scaled(hidden_in, attn_gain)
    def project(own, other, y_outer):
        part = reordered(normed, source_features(block_rows, y_outer, False))
        total = jnp.dot(part, own, preferred_element_type=jnp.float32)
        part = reordered(normed, source_features(block_rows, y_outer, True))
        return total + jnp.dot(part, other, preferred_element_type=jnp.float32)

    projected = jnp.concatenate(
        [project(first, first_other, True), project(last, last_other, False)], axis=1
    )
    half_size = HD // 2
    inverse = rope_base ** (-(jnp.arange(half_size, dtype=jnp.float32) * 2.0 / HD))
    angles = position.astype(jnp.float32)[:, None] * inverse[None, :]
    cosine = jnp.cos(angles)
    sine_part = jnp.sin(angles)
    keys_here = [
        rotated(projected[:, query_width + k * HD : query_width + (k + 1) * HD], cosine, sine_part)
        for k in range(KVH)
    ]
    values_here = projected[:, query_width + kv_width :].astype(jnp.bfloat16)
    kv_here = jnp.concatenate(keys_here + [values_here], axis=1)
    kv_group = spread(kv_here, CACHE, cache_size).reshape(group_rows, 2 * kv_width)
    queries = jnp.stack(
        [rotated(projected[:, h * HD : (h + 1) * HD], cosine, sine_part) for h in range(QH)]
    )
    allowed = (placing[None, :] >= prompt_start[:, None]) & (placing[None, :] <= my_place[:, None])
    contexts = []
    share = QH // KVH
    for k in range(KVH):
        key_head = kv_group[:, k * HD : (k + 1) * HD]
        value_head = kv_group[:, kv_width + k * HD : kv_width + (k + 1) * HD]
        scores = jnp.einsum(
            "htd,rd->htr",
            queries[k * share : (k + 1) * share],
            key_head,
            preferred_element_type=jnp.float32,
        ) * (HD ** (-0.5))
        scores = jnp.where(allowed[None], scores, masked_score)
        highest = jnp.max(scores, axis=-1, keepdims=True)
        weights = jnp.where(allowed[None], jnp.exp(scores - highest), 0.0)
        denominator = jnp.sum(weights, axis=-1, keepdims=True)
        numerator = jnp.einsum(
            "htr,rd->htd",
            weights.astype(jnp.bfloat16),
            value_head,
            preferred_element_type=jnp.float32,
        )
        contexts.append((numerator / denominator).astype(jnp.bfloat16))
    context = jnp.concatenate(contexts, axis=0)
    context = jnp.concatenate([context[h] for h in range(QH)], axis=1)
    attn_out = jnp.dot(context, full_out, preferred_element_type=jnp.float32)
    attended = (hidden_in.astype(jnp.float32) + attn_out).astype(jnp.bfloat16)
    moe_in = rms_scaled(attended, moe_gain)

    outgoing = jnp.dot(pick, moe_in, preferred_element_type=jnp.float32).astype(jnp.bfloat16)
    mine = lax.all_to_all(
        outgoing.reshape(CHIP_COUNT, MOST, model_width), CHIPS, 0, 0, tiled=True
    ).reshape(CHIP_COUNT * MOST, model_width)
    mates = lax.ppermute(mine, "core", CORES)
    gate_up = jnp.where(keep, w_gate_up[0], jnp.concatenate([other_low, other_high], axis=0))
    down_part = jnp.where(keep, w_down[0], other_down)
    for_mate = expert_half(mates, gate_up, down_part)
    from_mate = lax.ppermute(for_mate, "core", CORES)
    own_part = expert_half(mine, gate_up, down_part)
    expert_out = (own_part.astype(jnp.float32) + from_mate.astype(jnp.float32)).astype(jnp.bfloat16)
    returned = lax.all_to_all(
        expert_out.reshape(CHIP_COUNT, MOST, model_width), CHIPS, 0, 0, tiled=True
    ).reshape(CHIP_COUNT * MOST, model_width)
    blended = lax.dot_general(
        blend, returned, (((0,), (0,)), ((), ())), preferred_element_type=jnp.float32
    )
    mixture = blended[:row_count] + blended[row_count:]
    finished = (attended.astype(jnp.float32) + mixture).astype(jnp.bfloat16)

    home_rows = lax.all_to_all(
        finished.reshape(cache_size, deal_rows, model_width), CACHE, 0, 0, tiled=True
    ).reshape(row_count, model_width)
    my_base = group_base + my_index * row_count
    sender_place = lax.dynamic_slice_in_dim(
        placing.reshape(cache_size, row_count), my_index * deal_rows, deal_rows, axis=1
    ).reshape(-1)
    to_row = (sender_place[None, :] - my_base == row_ids[:, None]).astype(jnp.bfloat16)
    mixed = jnp.dot(to_row, home_rows, preferred_element_type=jnp.float32).astype(jnp.bfloat16)
    from_group = (placing[None, :] - my_base == row_ids[:, None]).astype(jnp.bfloat16)
    cached = jnp.dot(from_group, kv_group, preferred_element_type=jnp.float32).astype(jnp.bfloat16)
    return (mixed, cached[:, :kv_width], cached[:, kv_width:])


def solution(mesh):
    fine = Mesh(np.asarray(mesh.devices).reshape(tuple(SIZES[a] for a in ALL)), ALL)
    in_specs = (
        P(ALL, None),
        P(DP),
        P(ALL),
        P(),
        P(ALL, None),
        P(ALL, None),
        P(),
        P(ALL, None),
        P(ALL, None),
        P(ALL, None, None),
        P(ALL, None, None),
    )
    out_specs = (P(ALL, None), P(ALL, None), P(ALL, None))
    return jax.shard_map(
        per_device, mesh=fine, in_specs=in_specs, out_specs=out_specs, check_vma=False
    )
```

```python
import jax
import jax.numpy as jnp
import numpy as np
from jax import lax
from jax.experimental import pallas as pl
from jax.experimental.pallas import tpu as pltpu
from jax.sharding import Mesh
from jax.sharding import PartitionSpec as P

HD = 128
QH = 10
KVH = 2
TOP = 6
MOST = 16

DP = ("yh", "z", "core")
CACHE = ("yl", "x")
SIZES = {"yh": 2, "z": 4, "core": 2, "yl": 2, "x": 4}
ALL = DP + CACHE
CHIPS = ("yh", "z", "yl", "x")
CHIP_COUNT = 64

norm_eps = 1e-05
rope_base = 500000.0
masked_score = -1e30


def linear(yh, z, core, yl, x):
    return (((yh * 4 + z) * 2 + core) * 2 + yl) * 4 + x


def swap_pairs():
    pairs = []
    for yh in range(2):
        for z in range(4):
            for yl in range(2):
                for x in range(0, 4, 2):
                    low = linear(yh, z, 1, yl, x)
                    high = linear(yh, z, 0, yl, x + 1)
                    pairs += [(low, high), (high, low)]
    return pairs


def rms_scaled(features, gain_vector):
    widened = features.astype(jnp.float32)
    factor = lax.rsqrt(jnp.mean(widened * widened, axis=-1, keepdims=True) + norm_eps)
    return (widened * factor * gain_vector).astype(jnp.bfloat16)


def rotated(grouped, cosine, sine_part):
    half_size = HD // 2
    first_half = grouped[..., :half_size]
    second = grouped[..., half_size:]
    return jnp.concatenate(
        [first_half * cosine - second * sine_part, second * cosine + first_half * sine_part],
        axis=-1,
    ).astype(jnp.bfloat16)


def spread(shard, axes, count):
    return lax.all_to_all(
        jnp.broadcast_to(shard[None], (count,) + shard.shape), axes, 0, 0, tiled=True
    )


CORES = [(0, 1), (1, 0)]
ROW_TILE = 256
UP_CHUNK = 640


def expert_kernel(keep, rows, own_up, other_up, own_down, other_down, *rest):
    out, up, down, up_sems, down_sem = rest[-5:]
    up_chunks = up.shape[0] // UP_CHUNK
    half_size = up.shape[1] // 2

    def up_copy(i, mine):
        part = pl.ds(i * UP_CHUNK, UP_CHUNK)
        source = own_up if mine else other_up
        return pltpu.make_async_copy(source.at[part], up.at[part], up_sems.at[i])

    def down_copy(mine):
        return pltpu.make_async_copy(own_down if mine else other_down, down, down_sem)

    def finish(joined, wait):
        gate = joined[:, :half_size]
        active = (gate / (1.0 + jnp.exp(-gate)) * joined[:, half_size:]).astype(jnp.bfloat16)
        if wait:
            down_copy(True).wait()
        out[...] = jnp.dot(active, down[...], preferred_element_type=jnp.float32).astype(jnp.bfloat16)

    @pl.when(pl.program_id(0) == 0)
    def _():
        @pl.when(keep[0] == 1)
        def _():
            for i in range(up_chunks):
                up_copy(i, True).start()
            down_copy(True).start()

        @pl.when(keep[0] == 0)
        def _():
            for i in range(up_chunks):
                up_copy(i, False).start()
            down_copy(False).start()

        joined = jnp.zeros((rows.shape[0], up.shape[1]), jnp.float32)
        for i in range(up_chunks):
            up_copy(i, True).wait()
            part = slice(i * UP_CHUNK, (i + 1) * UP_CHUNK)
            joined = joined + jnp.dot(
                rows[:, part], up[part, :], preferred_element_type=jnp.float32
            )
        finish(joined, True)

    @pl.when(pl.program_id(0) != 0)
    def _():
        finish(jnp.dot(rows[...], up[...], preferred_element_type=jnp.float32), False)


def expert_half(keep, rows, weights, first, tiles, filled=None):
    own_up, _, own_down, _ = weights
    anywhere = pl.BlockSpec(memory_space=pl.ANY)
    tile = pl.BlockSpec((ROW_TILE, rows.shape[1]), lambda i, keep: (first + i, 0))
    extra = [] if filled is None else [filled]
    return pl.pallas_call(
        expert_kernel,
        out_shape=jax.ShapeDtypeStruct(rows.shape, jnp.bfloat16),
        grid_spec=pltpu.PrefetchScalarGridSpec(
            num_scalar_prefetch=1,
            grid=(tiles,),
            in_specs=[tile] + [anywhere] * (4 + len(extra)),
            out_specs=tile,
            scratch_shapes=[
                pltpu.VMEM(own_up.shape, jnp.bfloat16),
                pltpu.VMEM(own_down.shape, jnp.bfloat16),
                pltpu.SemaphoreType.DMA((own_up.shape[0] // UP_CHUNK,)),
                pltpu.SemaphoreType.DMA,
            ],
        ),
        input_output_aliases={} if filled is None else {6: 0},
        compiler_params=pltpu.CompilerParams(
            dimension_semantics=("arbitrary",), vmem_limit_bytes=50 << 20
        ),
        cost_estimate=pl.CostEstimate(
            flops=2 * tiles * ROW_TILE * (own_up.size + own_down.size),
            transcendentals=tiles * ROW_TILE * own_down.shape[0],
            bytes_accessed=2 * (own_up.size + own_down.size)
            + 4 * tiles * ROW_TILE * rows.shape[1],
        ),
    )(keep, rows, *weights, *extra)


def per_device(
    hidden_in,
    placing,
    prompt_start,
    attn_gain,
    w_qkv,
    w_out,
    moe_gain,
    routes,
    route_weight,
    w_gate_up,
    w_down,
):
    row_count, model_width = hidden_in.shape
    query_width = QH * HD
    kv_width = KVH * HD
    my_index = lax.axis_index(CACHE)
    group_rows = placing.shape[0]
    cache_size = group_rows // row_count
    deal_rows = row_count // cache_size
    group_base = lax.axis_index(DP) * group_rows

    pairs = swap_pairs()
    other_up = lax.ppermute(w_gate_up[0], ALL, pairs)
    other_down = lax.ppermute(w_down[0], ALL, pairs)
    keep = lax.axis_index("x") % 2 == lax.axis_index("core")

    qkv_rows = spread(w_qkv, CACHE, cache_size).reshape(-1, w_qkv.shape[1])
    kv_own = lax.all_gather(qkv_rows[:, query_width:], ("yh", "z"), axis=0, tiled=True)
    q_own = lax.all_gather(qkv_rows[:, :query_width], ("yh", "z"), axis=0, tiled=True)
    out_rows = spread(w_out, CACHE, cache_size).reshape(-1, w_out.shape[1])
    kv_own, out_rows = lax.optimization_barrier((kv_own, out_rows))
    out_own = lax.all_gather(out_rows, ("yh", "z"), axis=0, tiled=True)
    kv_other = lax.ppermute(kv_own, "core", CORES)

    my_place = lax.dynamic_slice_in_dim(placing, my_index * row_count, row_count)
    position = my_place - prompt_start

    bits = routes
    chip_of = (
        (bits & 0b111000)
        | ((bits & 0b000011) << 1)
        | ((bits & 0b000100) >> 2)
    )
    named = chip_of[:, :, None] == jnp.arange(CHIP_COUNT, dtype=jnp.int32)[None, None, :]
    member = jnp.any(named, axis=1)
    weight_of = jnp.sum(jnp.where(named, route_weight[:, :, None], 0.0), axis=1)
    row_ids = jnp.arange(row_count, dtype=jnp.int32)
    before = (row_ids[:, None] > row_ids[None, :]).astype(jnp.bfloat16)
    rank = jnp.dot(before, member.astype(jnp.bfloat16), preferred_element_type=jnp.float32)
    rank = jnp.where(member, rank.astype(jnp.int32), -1).T
    chosen = rank[:, None, :] == jnp.arange(MOST, dtype=jnp.int32)[None, :, None]
    chosen = chosen.reshape(CHIP_COUNT * MOST, row_count)
    pick = chosen.astype(jnp.bfloat16)
    weighted = jnp.where(
        chosen.reshape(CHIP_COUNT, MOST, row_count), weight_of.T[:, None, :], 0.0
    ).reshape(CHIP_COUNT * MOST, row_count)
    weighted_hi = lax.reduce_precision(weighted, 8, 7)
    weighted_lo = (weighted - weighted_hi).astype(jnp.bfloat16)
    blend = jnp.concatenate([weighted_hi.astype(jnp.bfloat16), weighted_lo], axis=1)

    normed = rms_scaled(hidden_in, attn_gain)
    by_core = normed.reshape(row_count, 8, 2, -1)
    by_core = [by_core[:, :, c].reshape(row_count, -1) for c in range(2)]
    core = lax.axis_index("core")
    normed_own = jnp.where(core == 0, by_core[0], by_core[1])
    normed_other = jnp.where(core == 0, by_core[1], by_core[0])
    normed_own, normed_other = lax.optimization_barrier((normed_own, normed_other))

    def project(own, other):
        total = jnp.dot(normed_own, own, preferred_element_type=jnp.float32)
        return total + jnp.dot(normed_other, other, preferred_element_type=jnp.float32)

    kv_projected = project(kv_own, kv_other)
    half_size = HD // 2
    inverse = rope_base ** (-(jnp.arange(half_size, dtype=jnp.float32) * 2.0 / HD))
    angles = position.astype(jnp.float32)[:, None] * inverse[None, :]
    cosine = jnp.cos(angles)
    sine_part = jnp.sin(angles)
    keys_here = [
        rotated(kv_projected[:, k * HD : (k + 1) * HD], cosine, sine_part)
        for k in range(KVH)
    ]
    values_here = kv_projected[:, kv_width:].astype(jnp.bfloat16)
    kv_here = jnp.concatenate(keys_here + [values_here], axis=1)
    kv_group = spread(kv_here, CACHE, cache_size).reshape(group_rows, 2 * kv_width)
    q_own, kv_group = lax.optimization_barrier((q_own, kv_group))
    q_other = lax.ppermute(q_own, "core", CORES)
    q_other, other_up = lax.optimization_barrier((q_other, other_up))
    projected = project(q_own, q_other)
    queries = jnp.stack(
        [rotated(projected[:, h * HD : (h + 1) * HD], cosine, sine_part) for h in range(QH)]
    )
    allowed = (placing[None, :] >= prompt_start[:, None]) & (placing[None, :] <= my_place[:, None])
    contexts = []
    share = QH // KVH
    for k in range(KVH):
        key_head = kv_group[:, k * HD : (k + 1) * HD]
        value_head = kv_group[:, kv_width + k * HD : kv_width + (k + 1) * HD]
        scores = jnp.einsum(
            "htd,rd->htr",
            queries[k * share : (k + 1) * share],
            key_head,
            preferred_element_type=jnp.float32,
        ) * (HD ** (-0.5))
        scores = jnp.where(allowed[None], scores, masked_score)
        highest = jnp.max(scores, axis=-1, keepdims=True)
        weights = jnp.where(allowed[None], jnp.exp(scores - highest), 0.0)
        denominator = jnp.sum(weights, axis=-1, keepdims=True)
        numerator = jnp.einsum(
            "htr,rd->htd",
            weights.astype(jnp.bfloat16),
            value_head,
            preferred_element_type=jnp.float32,
        )
        contexts.append((numerator / denominator).astype(jnp.bfloat16))
    context = jnp.concatenate(contexts, axis=0)
    context = jnp.concatenate([context[h] for h in range(QH)], axis=1)
    context, out_own, other_down = lax.optimization_barrier((context, out_own, other_down))
    out_other = lax.ppermute(out_own, "core", CORES)
    order = jnp.arange(query_width, dtype=jnp.int32)
    span = query_width // 2
    piece = w_out.shape[0] * cache_size
    at_core = jnp.where(order < span, core, 1 - core)
    inner = order % span
    source = (inner // piece * 2 + at_core) * piece + inner % piece
    take = (order[:, None] == source[None, :]).astype(jnp.bfloat16)
    take = lax.optimization_barrier(take)
    context = jnp.dot(context, take, preferred_element_type=jnp.float32).astype(jnp.bfloat16)
    attn_out = jnp.dot(context[:, :span], out_own, preferred_element_type=jnp.float32)
    attn_out = attn_out + jnp.dot(context[:, span:], out_other, preferred_element_type=jnp.float32)
    attended = (hidden_in.astype(jnp.float32) + attn_out).astype(jnp.bfloat16)
    moe_in = rms_scaled(attended, moe_gain)

    outgoing = jnp.dot(pick, moe_in, preferred_element_type=jnp.float32).astype(jnp.bfloat16)
    mine = lax.all_to_all(
        outgoing.reshape(CHIP_COUNT, MOST, model_width), CHIPS, 0, 0, tiled=True
    ).reshape(CHIP_COUNT * MOST, model_width)
    mates = lax.ppermute(mine, "core", CORES)
    weights = (w_gate_up[0], other_up, w_down[0], other_down)
    kept = keep.astype(jnp.int32).reshape(1)
    tiles = mine.shape[0] // ROW_TILE
    own_part = expert_half(kept, mine, weights, 0, tiles // 2)
    mates, own_part = lax.optimization_barrier((mates, own_part))
    for_mate = expert_half(kept, mates, weights, 0, tiles)
    from_mate = lax.ppermute(for_mate, "core", CORES)
    own_part = expert_half(kept, mine, weights, tiles // 2, tiles // 2, own_part)
    expert_out = (own_part.astype(jnp.float32) + from_mate.astype(jnp.float32)).astype(jnp.bfloat16)
    returned = lax.all_to_all(
        expert_out.reshape(CHIP_COUNT, MOST, model_width), CHIPS, 0, 0, tiled=True
    ).reshape(CHIP_COUNT * MOST, model_width)
    blended = lax.dot_general(
        blend, returned, (((0,), (0,)), ((), ())), preferred_element_type=jnp.float32
    )
    mixture = blended[:row_count] + blended[row_count:]
    finished = (attended.astype(jnp.float32) + mixture).astype(jnp.bfloat16)

    home_rows = lax.all_to_all(
        finished.reshape(cache_size, deal_rows, model_width), CACHE, 0, 0, tiled=True
    ).reshape(row_count, model_width)
    my_base = group_base + my_index * row_count
    sender_place = lax.dynamic_slice_in_dim(
        placing.reshape(cache_size, row_count), my_index * deal_rows, deal_rows, axis=1
    ).reshape(-1)
    to_row = (sender_place[None, :] - my_base == row_ids[:, None]).astype(jnp.bfloat16)
    mixed = jnp.dot(to_row, home_rows, preferred_element_type=jnp.float32).astype(jnp.bfloat16)
    from_group = (placing[None, :] - my_base == row_ids[:, None]).astype(jnp.bfloat16)
    cached = jnp.dot(from_group, kv_group, preferred_element_type=jnp.float32).astype(jnp.bfloat16)
    return (mixed, cached[:, :kv_width], cached[:, kv_width:])


def solution(mesh):
    fine = Mesh(np.asarray(mesh.devices).reshape(tuple(SIZES[a] for a in ALL)), ALL)
    in_specs = (
        P(ALL, None),
        P(DP),
        P(ALL),
        P(),
        P(ALL, None),
        P(ALL, None),
        P(),
        P(ALL, None),
        P(ALL, None),
        P(ALL, None, None),
        P(ALL, None, None),
    )
    out_specs = (P(ALL, None), P(ALL, None), P(ALL, None))
    return jax.shard_map(
        per_device, mesh=fine, in_specs=in_specs, out_specs=out_specs, check_vma=False
    )
```

```python
import jax
import jax.numpy as jnp
import numpy as np
from jax import lax
from jax.experimental import pallas as pl
from jax.experimental.pallas import tpu as pltpu
from jax.sharding import Mesh
from jax.sharding import PartitionSpec as P

HD = 128
QH = 10
KVH = 2
TOP = 6
MOST = 16

DP = ("yh", "z", "core")
CACHE = ("yl", "x")
SIZES = {"yh": 2, "z": 4, "core": 2, "yl": 2, "x": 4}
ALL = DP + CACHE
CHIPS = ("yh", "z", "yl", "x")
CHIP_COUNT = 64

norm_eps = 1e-05
rope_base = 500000.0
masked_score = -1e30


def linear(yh, z, core, yl, x):
    return (((yh * 4 + z) * 2 + core) * 2 + yl) * 4 + x


def swap_pairs():
    pairs = []
    for yh in range(2):
        for z in range(4):
            for yl in range(2):
                for x in range(0, 4, 2):
                    low = linear(yh, z, 1, yl, x)
                    high = linear(yh, z, 0, yl, x + 1)
                    pairs += [(low, high), (high, low)]
    return pairs


def rms_scaled(features, gain_vector):
    widened = features.astype(jnp.float32)
    factor = lax.rsqrt(jnp.mean(widened * widened, axis=-1, keepdims=True) + norm_eps)
    return (widened * factor * gain_vector).astype(jnp.bfloat16)


def rotated(grouped, cosine, sine_part):
    half_size = HD // 2
    first_half = grouped[..., :half_size]
    second = grouped[..., half_size:]
    return jnp.concatenate(
        [first_half * cosine - second * sine_part, second * cosine + first_half * sine_part],
        axis=-1,
    ).astype(jnp.bfloat16)


def spread(shard, axes, count):
    return lax.all_to_all(
        jnp.broadcast_to(shard[None], (count,) + shard.shape), axes, 0, 0, tiled=True
    )


CORES = [(0, 1), (1, 0)]
ROW_TILE = 256
UP_CHUNK = 640


def expert_kernel(keep, rows, own_up, other_up, own_down, other_down, *rest):
    out, up, down, up_sems, down_sem = rest[-5:]
    up_chunks = up.shape[0] // UP_CHUNK
    half_size = up.shape[1] // 2

    def up_copy(i, mine):
        part = pl.ds(i * UP_CHUNK, UP_CHUNK)
        source = own_up if mine else other_up
        return pltpu.make_async_copy(source.at[part], up.at[part], up_sems.at[i])

    def down_copy(mine):
        return pltpu.make_async_copy(own_down if mine else other_down, down, down_sem)

    def finish(joined, wait):
        gate = joined[:, :half_size]
        active = (gate / (1.0 + jnp.exp(-gate)) * joined[:, half_size:]).astype(jnp.bfloat16)
        if wait:
            down_copy(True).wait()
        out[...] = jnp.dot(active, down[...], preferred_element_type=jnp.float32).astype(jnp.bfloat16)

    @pl.when(pl.program_id(0) == 0)
    def _():
        @pl.when(keep[0] == 1)
        def _():
            for i in range(up_chunks):
                up_copy(i, True).start()
            down_copy(True).start()

        @pl.when(keep[0] == 0)
        def _():
            for i in range(up_chunks):
                up_copy(i, False).start()
            down_copy(False).start()

        joined = jnp.zeros((rows.shape[0], up.shape[1]), jnp.float32)
        for i in range(up_chunks):
            up_copy(i, True).wait()
            part = slice(i * UP_CHUNK, (i + 1) * UP_CHUNK)
            joined = joined + jnp.dot(
                rows[:, part], up[part, :], preferred_element_type=jnp.float32
            )
        finish(joined, True)

    @pl.when(pl.program_id(0) != 0)
    def _():
        finish(jnp.dot(rows[...], up[...], preferred_element_type=jnp.float32), False)


def expert_half(keep, rows, weights, first, tiles, filled=None):
    own_up, _, own_down, _ = weights
    anywhere = pl.BlockSpec(memory_space=pl.ANY)
    tile = pl.BlockSpec((ROW_TILE, rows.shape[1]), lambda i, keep: (first + i, 0))
    extra = [] if filled is None else [filled]
    return pl.pallas_call(
        expert_kernel,
        out_shape=jax.ShapeDtypeStruct(rows.shape, jnp.bfloat16),
        grid_spec=pltpu.PrefetchScalarGridSpec(
            num_scalar_prefetch=1,
            grid=(tiles,),
            in_specs=[tile] + [anywhere] * (4 + len(extra)),
            out_specs=tile,
            scratch_shapes=[
                pltpu.VMEM(own_up.shape, jnp.bfloat16),
                pltpu.VMEM(own_down.shape, jnp.bfloat16),
                pltpu.SemaphoreType.DMA((own_up.shape[0] // UP_CHUNK,)),
                pltpu.SemaphoreType.DMA,
            ],
        ),
        input_output_aliases={} if filled is None else {6: 0},
        compiler_params=pltpu.CompilerParams(
            dimension_semantics=("arbitrary",), vmem_limit_bytes=50 << 20
        ),
        cost_estimate=pl.CostEstimate(
            flops=2 * tiles * ROW_TILE * (own_up.size + own_down.size),
            transcendentals=tiles * ROW_TILE * own_down.shape[0],
            bytes_accessed=2 * (own_up.size + own_down.size)
            + 4 * tiles * ROW_TILE * rows.shape[1],
        ),
    )(keep, rows, *weights, *extra)


def per_device(
    hidden_in,
    placing,
    prompt_start,
    attn_gain,
    w_qkv,
    w_out,
    moe_gain,
    routes,
    route_weight,
    w_gate_up,
    w_down,
):
    row_count, model_width = hidden_in.shape
    query_width = QH * HD
    kv_width = KVH * HD
    my_index = lax.axis_index(CACHE)
    group_rows = placing.shape[0]
    cache_size = group_rows // row_count
    deal_rows = row_count // cache_size
    group_base = lax.axis_index(DP) * group_rows

    half_out = w_out.shape[1] // 2
    joint = jnp.concatenate(
        [w_qkv, jnp.concatenate([w_out[:, :half_out], w_out[:, half_out:]], axis=0)], axis=1
    )
    joint = spread(joint, CACHE, cache_size)
    qkv_rows = joint[:, :, : w_qkv.shape[1]].reshape(-1, w_qkv.shape[1])
    halves = joint[:, :, w_qkv.shape[1] :].reshape(cache_size, 2, w_out.shape[0], half_out)
    out_rows = jnp.concatenate([halves[:, 0], halves[:, 1]], axis=2).reshape(-1, w_out.shape[1])

    pairs = swap_pairs()
    sent_up, qkv_rows, out_rows = lax.optimization_barrier((w_gate_up[0], qkv_rows, out_rows))
    other_up = lax.ppermute(sent_up, ALL, pairs)
    keep = lax.axis_index("x") % 2 == lax.axis_index("core")

    full_qkv = lax.all_gather(qkv_rows, DP, axis=0, tiled=True)
    out_own = spread(out_rows, ("yh", "z"), 8).reshape(-1, w_out.shape[1])
    out_other = lax.ppermute(out_own, "core", CORES)
    full_qkv, other_up, out_own = lax.optimization_barrier((full_qkv, other_up, out_own))

    my_place = lax.dynamic_slice_in_dim(placing, my_index * row_count, row_count)
    position = my_place - prompt_start

    bits = routes
    chip_of = (
        (bits & 0b111000)
        | ((bits & 0b000011) << 1)
        | ((bits & 0b000100) >> 2)
    )
    named = chip_of[:, :, None] == jnp.arange(CHIP_COUNT, dtype=jnp.int32)[None, None, :]
    member = jnp.any(named, axis=1)
    weight_of = jnp.sum(jnp.where(named, route_weight[:, :, None], 0.0), axis=1)
    row_ids = jnp.arange(row_count, dtype=jnp.int32)
    before = (row_ids[:, None] > row_ids[None, :]).astype(jnp.bfloat16)
    rank = jnp.dot(before, member.astype(jnp.bfloat16), preferred_element_type=jnp.float32)
    rank = jnp.where(member, rank.astype(jnp.int32), -1).T
    chosen = rank[:, None, :] == jnp.arange(MOST, dtype=jnp.int32)[None, :, None]
    chosen = chosen.reshape(CHIP_COUNT * MOST, row_count)
    pick = chosen.astype(jnp.bfloat16)
    weighted = jnp.where(
        chosen.reshape(CHIP_COUNT, MOST, row_count), weight_of.T[:, None, :], 0.0
    ).reshape(CHIP_COUNT * MOST, row_count)
    weighted_hi = lax.reduce_precision(weighted, 8, 7)
    weighted_lo = (weighted - weighted_hi).astype(jnp.bfloat16)
    blend = jnp.concatenate([weighted_hi.astype(jnp.bfloat16), weighted_lo], axis=1)

    normed = rms_scaled(hidden_in, attn_gain)
    core = lax.axis_index("core")
    projected = jnp.dot(normed, full_qkv, preferred_element_type=jnp.float32)
    half_size = HD // 2
    inverse = rope_base ** (-(jnp.arange(half_size, dtype=jnp.float32) * 2.0 / HD))
    angles = position.astype(jnp.float32)[:, None] * inverse[None, :]
    cosine = jnp.cos(angles)
    sine_part = jnp.sin(angles)
    keys_here = [
        rotated(projected[:, query_width + k * HD : query_width + (k + 1) * HD], cosine, sine_part)
        for k in range(KVH)
    ]
    values_here = projected[:, query_width + kv_width :].astype(jnp.bfloat16)
    kv_here = jnp.concatenate(keys_here + [values_here], axis=1)
    kv_group = spread(kv_here, CACHE, cache_size).reshape(group_rows, 2 * kv_width)
    kv_group, sent_down = lax.optimization_barrier((kv_group, w_down[0]))
    other_down = lax.ppermute(sent_down, ALL, pairs)
    queries = jnp.stack(
        [rotated(projected[:, h * HD : (h + 1) * HD], cosine, sine_part) for h in range(QH)]
    )
    allowed = (placing[None, :] >= prompt_start[:, None]) & (placing[None, :] <= my_place[:, None])
    contexts = []
    share = QH // KVH
    for k in range(KVH):
        key_head = kv_group[:, k * HD : (k + 1) * HD]
        value_head = kv_group[:, kv_width + k * HD : kv_width + (k + 1) * HD]
        scores = jnp.einsum(
            "htd,rd->htr",
            queries[k * share : (k + 1) * share],
            key_head,
            preferred_element_type=jnp.float32,
        ) * (HD ** (-0.5))
        scores = jnp.where(allowed[None], scores, masked_score)
        highest = jnp.max(scores, axis=-1, keepdims=True)
        weights = jnp.where(allowed[None], jnp.exp(scores - highest), 0.0)
        denominator = jnp.sum(weights, axis=-1, keepdims=True)
        numerator = jnp.einsum(
            "htr,rd->htd",
            weights.astype(jnp.bfloat16),
            value_head,
            preferred_element_type=jnp.float32,
        )
        contexts.append((numerator / denominator).astype(jnp.bfloat16))
    context = jnp.concatenate(contexts, axis=0)
    context = jnp.concatenate([context[h] for h in range(QH)], axis=1)
    order = jnp.arange(query_width, dtype=jnp.int32)
    span = query_width // 2
    piece = w_out.shape[0] * cache_size
    at_core = jnp.where(order < span, core, 1 - core)
    inner = order % span
    source = (inner // piece * 2 + at_core) * piece + inner % piece
    take = (order[:, None] == source[None, :]).astype(jnp.bfloat16)
    take = lax.optimization_barrier(take)
    context = jnp.dot(context, take, preferred_element_type=jnp.float32).astype(jnp.bfloat16)
    attn_out = jnp.dot(context[:, :span], out_own, preferred_element_type=jnp.float32)
    attn_out = attn_out + jnp.dot(context[:, span:], out_other, preferred_element_type=jnp.float32)
    attended = (hidden_in.astype(jnp.float32) + attn_out).astype(jnp.bfloat16)
    moe_in = rms_scaled(attended, moe_gain)

    outgoing = jnp.dot(pick, moe_in, preferred_element_type=jnp.float32).astype(jnp.bfloat16)
    outgoing, other_down = lax.optimization_barrier((outgoing, other_down))
    mine = lax.all_to_all(
        outgoing.reshape(CHIP_COUNT, MOST, model_width), CHIPS, 0, 0, tiled=True
    ).reshape(CHIP_COUNT * MOST, model_width)
    mates = lax.ppermute(mine, "core", CORES)
    weights = (w_gate_up[0], other_up, w_down[0], other_down)
    kept = keep.astype(jnp.int32).reshape(1)
    tiles = mine.shape[0] // ROW_TILE
    own_part = expert_half(kept, mine, weights, 0, tiles // 2)
    mates, own_part = lax.optimization_barrier((mates, own_part))
    for_mate = expert_half(kept, mates, weights, 0, tiles)
    from_mate = lax.ppermute(for_mate, "core", CORES)
    own_part = expert_half(kept, mine, weights, tiles // 2, tiles // 2, own_part)
    expert_out = (own_part.astype(jnp.float32) + from_mate.astype(jnp.float32)).astype(jnp.bfloat16)
    returned = lax.all_to_all(
        expert_out.reshape(CHIP_COUNT, MOST, model_width), CHIPS, 0, 0, tiled=True
    ).reshape(CHIP_COUNT * MOST, model_width)
    blended = lax.dot_general(
        blend, returned, (((0,), (0,)), ((), ())), preferred_element_type=jnp.float32
    )
    mixture = blended[:row_count] + blended[row_count:]
    finished = (attended.astype(jnp.float32) + mixture).astype(jnp.bfloat16)

    home_rows = lax.all_to_all(
        finished.reshape(cache_size, deal_rows, model_width), CACHE, 0, 0, tiled=True
    ).reshape(row_count, model_width)
    my_base = group_base + my_index * row_count
    sender_place = lax.dynamic_slice_in_dim(
        placing.reshape(cache_size, row_count), my_index * deal_rows, deal_rows, axis=1
    ).reshape(-1)
    to_row = (sender_place[None, :] - my_base == row_ids[:, None]).astype(jnp.bfloat16)
    mixed = jnp.dot(to_row, home_rows, preferred_element_type=jnp.float32).astype(jnp.bfloat16)
    from_group = (placing[None, :] - my_base == row_ids[:, None]).astype(jnp.bfloat16)
    cached = jnp.dot(from_group, kv_group, preferred_element_type=jnp.float32).astype(jnp.bfloat16)
    return (mixed, cached[:, :kv_width], cached[:, kv_width:])


def solution(mesh):
    fine = Mesh(np.asarray(mesh.devices).reshape(tuple(SIZES[a] for a in ALL)), ALL)
    in_specs = (
        P(ALL, None),
        P(DP),
        P(ALL),
        P(),
        P(ALL, None),
        P(ALL, None),
        P(),
        P(ALL, None),
        P(ALL, None),
        P(ALL, None, None),
        P(ALL, None, None),
    )
    out_specs = (P(ALL, None), P(ALL, None), P(ALL, None))
    return jax.shard_map(
        per_device, mesh=fine, in_specs=in_specs, out_specs=out_specs, check_vma=False
    )
```

```python
import jax
import jax.numpy as jnp
import numpy as np
from jax import lax
from jax.experimental import pallas as pl
from jax.experimental.pallas import tpu as pltpu
from jax.sharding import Mesh
from jax.sharding import PartitionSpec as P

HD = 128
QH = 10
KVH = 2
TOP = 6
MOST = 16

DP = ("yh", "z", "core")
CACHE = ("yl", "x")
SIZES = {"yh": 2, "z": 4, "core": 2, "yl": 2, "x": 4}
ALL = DP + CACHE
CHIPS = ("yh", "z", "yl", "x")
CHIP_COUNT = 64

norm_eps = 1e-05
rope_base = 500000.0
masked_score = -1e30


def linear(yh, z, core, yl, x):
    return (((yh * 4 + z) * 2 + core) * 2 + yl) * 4 + x


def swap_pairs():
    pairs = []
    for yh in range(2):
        for z in range(4):
            for yl in range(2):
                for x in range(0, 4, 2):
                    low = linear(yh, z, 1, yl, x)
                    high = linear(yh, z, 0, yl, x + 1)
                    pairs += [(low, high), (high, low)]
    return pairs


def rms_scaled(features, gain_vector):
    widened = features.astype(jnp.float32)
    factor = lax.rsqrt(jnp.mean(widened * widened, axis=-1, keepdims=True) + norm_eps)
    return (widened * factor * gain_vector).astype(jnp.bfloat16)


def turned(head, cosines, sines):
    return (head * cosines + pltpu.roll(head, HD // 2, 1) * sines).astype(jnp.bfloat16)


def keys_values_kernel(normed, w_block, cosines, sines, out):
    block = jnp.dot(normed[...], w_block[...], preferred_element_type=jnp.float32)

    def write(columns, part):
        for copy in range(out.shape[0]):
            out[copy, :, columns] = part

    @pl.when(pl.program_id(0) == 0)
    def _():
        for k in range(KVH):
            columns = slice(k * HD, (k + 1) * HD)
            write(columns, turned(block[:, columns], cosines[...], sines[...]))

    @pl.when(pl.program_id(0) == 1)
    def _():
        write(slice(0, KVH * HD), block.astype(jnp.bfloat16))


def keys_values(normed, w_qkv, cosines, sines, copies):
    row_count, model_width = normed.shape
    width = KVH * HD
    whole = lambda i: (0, 0)
    return pl.pallas_call(
        keys_values_kernel,
        out_shape=jax.ShapeDtypeStruct((copies, row_count, 2 * width), jnp.bfloat16),
        grid=(2,),
        in_specs=[
            pl.BlockSpec((row_count, model_width), whole),
            pl.BlockSpec((model_width, width), lambda i: (0, QH * HD // width + i)),
            pl.BlockSpec((row_count, HD), whole),
            pl.BlockSpec((row_count, HD), whole),
        ],
        out_specs=pl.BlockSpec((copies, row_count, width), lambda i: (0, 0, i)),
        compiler_params=pltpu.CompilerParams(
            dimension_semantics=("arbitrary",), vmem_limit_bytes=32 << 20
        ),
    )(normed, w_qkv, cosines, sines)


def attention_kernel(projected, cosines, sines, kv_group, placing, start, place, out):
    allowed = (placing[...] >= start[...]) & (placing[...] <= place[...])
    share = QH // KVH
    for h in range(QH):
        columns = slice(h * HD, (h + 1) * HD)
        k = h // share
        query = turned(projected[:, columns], cosines[...], sines[...])
        scores = lax.dot_general(
            query,
            kv_group[:, k * HD : (k + 1) * HD],
            (((1,), (1,)), ((), ())),
            preferred_element_type=jnp.float32,
        ) * (HD ** (-0.5))
        scores = jnp.where(allowed, scores, masked_score)
        highest = jnp.max(scores, axis=1, keepdims=True)
        weights = jnp.where(allowed, jnp.exp(scores - highest), 0.0)
        denominator = jnp.sum(weights, axis=1, keepdims=True)
        numerator = jnp.dot(
            weights.astype(jnp.bfloat16),
            kv_group[:, (KVH + k) * HD : (KVH + k + 1) * HD],
            preferred_element_type=jnp.float32,
        )
        out[:, columns] = (numerator / denominator).astype(jnp.bfloat16)


def attention(projected, *operands):
    return pl.pallas_call(
        attention_kernel,
        out_shape=jax.ShapeDtypeStruct(projected.shape, jnp.bfloat16),
        compiler_params=pltpu.CompilerParams(vmem_limit_bytes=32 << 20),
    )(projected, *operands)


def spread(shard, axes, count):
    return lax.all_to_all(
        jnp.broadcast_to(shard[None], (count,) + shard.shape), axes, 0, 0, tiled=True
    )


CORES = [(0, 1), (1, 0)]
ROW_TILE = 256
UP_CHUNK = 640


def expert_kernel(keep, rows, own_up, other_up, own_down, other_down, *rest):
    out, up, down, up_sems, down_sem = rest[-5:]
    up_chunks = up.shape[0] // UP_CHUNK
    half_size = up.shape[1] // 2

    def up_copy(i, mine):
        part = pl.ds(i * UP_CHUNK, UP_CHUNK)
        source = own_up if mine else other_up
        return pltpu.make_async_copy(source.at[part], up.at[part], up_sems.at[i])

    def down_copy(mine):
        return pltpu.make_async_copy(own_down if mine else other_down, down, down_sem)

    def finish(joined, wait):
        gate = joined[:, :half_size]
        active = (gate / (1.0 + jnp.exp(-gate)) * joined[:, half_size:]).astype(jnp.bfloat16)
        if wait:
            down_copy(True).wait()
        out[...] = jnp.dot(active, down[...], preferred_element_type=jnp.float32).astype(jnp.bfloat16)

    @pl.when(pl.program_id(0) == 0)
    def _():
        @pl.when(keep[0] == 1)
        def _():
            for i in range(up_chunks):
                up_copy(i, True).start()
            down_copy(True).start()

        @pl.when(keep[0] == 0)
        def _():
            for i in range(up_chunks):
                up_copy(i, False).start()
            down_copy(False).start()

        joined = jnp.zeros((rows.shape[0], up.shape[1]), jnp.float32)
        for i in range(up_chunks):
            up_copy(i, True).wait()
            part = slice(i * UP_CHUNK, (i + 1) * UP_CHUNK)
            joined = joined + jnp.dot(
                rows[:, part], up[part, :], preferred_element_type=jnp.float32
            )
        finish(joined, True)

    @pl.when(pl.program_id(0) != 0)
    def _():
        finish(jnp.dot(rows[...], up[...], preferred_element_type=jnp.float32), False)


def expert_half(keep, rows, weights, first, tiles, filled=None):
    own_up, _, own_down, _ = weights
    anywhere = pl.BlockSpec(memory_space=pl.ANY)
    tile = pl.BlockSpec((ROW_TILE, rows.shape[1]), lambda i, keep: (first + i, 0))
    extra = [] if filled is None else [filled]
    return pl.pallas_call(
        expert_kernel,
        out_shape=jax.ShapeDtypeStruct(rows.shape, jnp.bfloat16),
        grid_spec=pltpu.PrefetchScalarGridSpec(
            num_scalar_prefetch=1,
            grid=(tiles,),
            in_specs=[tile] + [anywhere] * (4 + len(extra)),
            out_specs=tile,
            scratch_shapes=[
                pltpu.VMEM(own_up.shape, jnp.bfloat16),
                pltpu.VMEM(own_down.shape, jnp.bfloat16),
                pltpu.SemaphoreType.DMA((own_up.shape[0] // UP_CHUNK,)),
                pltpu.SemaphoreType.DMA,
            ],
        ),
        input_output_aliases={} if filled is None else {6: 0},
        compiler_params=pltpu.CompilerParams(
            dimension_semantics=("arbitrary",), vmem_limit_bytes=50 << 20
        ),
        cost_estimate=pl.CostEstimate(
            flops=2 * tiles * ROW_TILE * (own_up.size + own_down.size),
            transcendentals=tiles * ROW_TILE * own_down.shape[0],
            bytes_accessed=2 * (own_up.size + own_down.size)
            + 4 * tiles * ROW_TILE * rows.shape[1],
        ),
    )(keep, rows, *weights, *extra)


def per_device(
    hidden_in,
    placing,
    prompt_start,
    attn_gain,
    w_qkv,
    w_out,
    moe_gain,
    routes,
    route_weight,
    w_gate_up,
    w_down,
):
    row_count, model_width = hidden_in.shape
    query_width = QH * HD
    kv_width = KVH * HD
    my_index = lax.axis_index(CACHE)
    group_rows = placing.shape[0]
    cache_size = group_rows // row_count
    deal_rows = row_count // cache_size
    group_base = lax.axis_index(DP) * group_rows

    half_out = w_out.shape[1] // 2
    joint = jnp.concatenate(
        [w_qkv, jnp.concatenate([w_out[:, :half_out], w_out[:, half_out:]], axis=0)], axis=1
    )
    joint = spread(joint, CACHE, cache_size)
    qkv_rows = joint[:, :, : w_qkv.shape[1]].reshape(-1, w_qkv.shape[1])
    halves = joint[:, :, w_qkv.shape[1] :].reshape(cache_size, 2, w_out.shape[0], half_out)
    out_rows = jnp.concatenate([halves[:, 0], halves[:, 1]], axis=2).reshape(-1, w_out.shape[1])

    pairs = swap_pairs()
    sent_up, qkv_rows, out_rows = lax.optimization_barrier((w_gate_up[0], qkv_rows, out_rows))
    other_up = lax.ppermute(sent_up, ALL, pairs)
    keep = lax.axis_index("x") % 2 == lax.axis_index("core")

    full_qkv = lax.all_gather(qkv_rows, DP, axis=0, tiled=True)
    full_out = lax.all_gather(out_rows, DP, axis=0, tiled=True)
    full_qkv, other_up = lax.optimization_barrier((full_qkv, other_up))

    my_place = lax.dynamic_slice_in_dim(placing, my_index * row_count, row_count)
    position = my_place - prompt_start

    bits = routes
    chip_of = (
        (bits & 0b111000)
        | ((bits & 0b000011) << 1)
        | ((bits & 0b000100) >> 2)
    )
    named = chip_of[:, :, None] == jnp.arange(CHIP_COUNT, dtype=jnp.int32)[None, None, :]
    member = jnp.any(named, axis=1)
    weight_of = jnp.sum(jnp.where(named, route_weight[:, :, None], 0.0), axis=1)
    row_ids = jnp.arange(row_count, dtype=jnp.int32)
    before = (row_ids[:, None] > row_ids[None, :]).astype(jnp.bfloat16)
    rank = jnp.dot(before, member.astype(jnp.bfloat16), preferred_element_type=jnp.float32)
    rank = jnp.where(member, rank.astype(jnp.int32), -1).T
    chosen = rank[:, None, :] == jnp.arange(MOST, dtype=jnp.int32)[None, :, None]
    chosen = chosen.reshape(CHIP_COUNT * MOST, row_count)
    pick = chosen.astype(jnp.bfloat16)
    weighted = jnp.where(
        chosen.reshape(CHIP_COUNT, MOST, row_count), weight_of.T[:, None, :], 0.0
    ).reshape(CHIP_COUNT * MOST, row_count)
    weighted_hi = lax.reduce_precision(weighted, 8, 7)
    weighted_lo = (weighted - weighted_hi).astype(jnp.bfloat16)
    blend = jnp.concatenate([weighted_hi.astype(jnp.bfloat16), weighted_lo], axis=1)

    normed = rms_scaled(hidden_in, attn_gain)
    half_size = HD // 2
    inverse = rope_base ** (-(jnp.arange(half_size, dtype=jnp.float32) * 2.0 / HD))
    angles = position.astype(jnp.float32)[:, None] * inverse[None, :]
    cosine = jnp.cos(angles)
    sine_part = jnp.sin(angles)
    cosines = jnp.concatenate([cosine, cosine], axis=1)
    sines = jnp.concatenate([-sine_part, sine_part], axis=1)
    kv_copies = keys_values(normed, full_qkv, cosines, sines, cache_size)
    kv_group = lax.all_to_all(kv_copies, CACHE, 0, 0, tiled=True).reshape(group_rows, 2 * kv_width)
    projected = jnp.dot(normed, full_qkv[:, :query_width], preferred_element_type=jnp.float32)
    kv_group, projected, sent_down = lax.optimization_barrier((kv_group, projected, w_down[0]))
    other_down = lax.ppermute(sent_down, ALL, pairs)
    context = attention(
        projected, cosines, sines, kv_group, placing[None, :], prompt_start[:, None], my_place[:, None]
    )
    attn_out = jnp.dot(context, full_out, preferred_element_type=jnp.float32)
    attended = (hidden_in.astype(jnp.float32) + attn_out).astype(jnp.bfloat16)
    moe_in = rms_scaled(attended, moe_gain)

    outgoing = jnp.dot(pick, moe_in, preferred_element_type=jnp.float32).astype(jnp.bfloat16)
    outgoing, other_down = lax.optimization_barrier((outgoing, other_down))
    mine = lax.all_to_all(
        outgoing.reshape(CHIP_COUNT, MOST, model_width), CHIPS, 0, 0, tiled=True
    ).reshape(CHIP_COUNT * MOST, model_width)
    mates = lax.ppermute(mine, "core", CORES)
    weights = (w_gate_up[0], other_up, w_down[0], other_down)
    kept = keep.astype(jnp.int32).reshape(1)
    tiles = mine.shape[0] // ROW_TILE
    own_part = expert_half(kept, mine, weights, 0, tiles // 2)
    mates, own_part = lax.optimization_barrier((mates, own_part))
    for_mate = expert_half(kept, mates, weights, 0, tiles)
    from_mate = lax.ppermute(for_mate, "core", CORES)
    own_part = expert_half(kept, mine, weights, tiles // 2, tiles // 2, own_part)
    expert_out = (own_part.astype(jnp.float32) + from_mate.astype(jnp.float32)).astype(jnp.bfloat16)
    returned = lax.all_to_all(
        expert_out.reshape(CHIP_COUNT, MOST, model_width), CHIPS, 0, 0, tiled=True
    ).reshape(CHIP_COUNT * MOST, model_width)
    blended = lax.dot_general(
        blend, returned, (((0,), (0,)), ((), ())), preferred_element_type=jnp.float32
    )
    mixture = blended[:row_count] + blended[row_count:]
    finished = (attended.astype(jnp.float32) + mixture).astype(jnp.bfloat16)

    home_rows = lax.all_to_all(
        finished.reshape(cache_size, deal_rows, model_width), CACHE, 0, 0, tiled=True
    ).reshape(row_count, model_width)
    my_base = group_base + my_index * row_count
    sender_place = lax.dynamic_slice_in_dim(
        placing.reshape(cache_size, row_count), my_index * deal_rows, deal_rows, axis=1
    ).reshape(-1)
    to_row = (sender_place[None, :] - my_base == row_ids[:, None]).astype(jnp.bfloat16)
    mixed = jnp.dot(to_row, home_rows, preferred_element_type=jnp.float32).astype(jnp.bfloat16)
    from_group = (placing[None, :] - my_base == row_ids[:, None]).astype(jnp.bfloat16)
    cached = jnp.dot(from_group, kv_group, preferred_element_type=jnp.float32).astype(jnp.bfloat16)
    return (mixed, cached[:, :kv_width], cached[:, kv_width:])


def solution(mesh):
    fine = Mesh(np.asarray(mesh.devices).reshape(tuple(SIZES[a] for a in ALL)), ALL)
    in_specs = (
        P(ALL, None),
        P(DP),
        P(ALL),
        P(),
        P(ALL, None),
        P(ALL, None),
        P(),
        P(ALL, None),
        P(ALL, None),
        P(ALL, None, None),
        P(ALL, None, None),
    )
    out_specs = (P(ALL, None), P(ALL, None), P(ALL, None))
    return jax.shard_map(
        per_device, mesh=fine, in_specs=in_specs, out_specs=out_specs, check_vma=False
    )
```

```python
import jax
import jax.numpy as jnp
import numpy as np
from jax import lax
from jax.experimental import pallas as pl
from jax.experimental.pallas import tpu as pltpu
from jax.sharding import Mesh
from jax.sharding import PartitionSpec as P

HD = 128
QH = 10
KVH = 2
TOP = 6
MOST = 16

DP = ("yh", "z", "core")
CACHE = ("yl", "x")
SIZES = {"yh": 2, "z": 4, "core": 2, "yl": 2, "x": 4}
ALL = DP + CACHE
CHIPS = ("yh", "z", "yl", "x")
CHIP_COUNT = 64

norm_eps = 1e-05
rope_base = 500000.0
masked_score = -1e30


def linear(yh, z, core, yl, x):
    return (((yh * 4 + z) * 2 + core) * 2 + yl) * 4 + x


def swap_pairs():
    pairs = []
    for yh in range(2):
        for z in range(4):
            for yl in range(2):
                for x in range(0, 4, 2):
                    low = linear(yh, z, 1, yl, x)
                    high = linear(yh, z, 0, yl, x + 1)
                    pairs += [(low, high), (high, low)]
    return pairs


def rms_scaled(features, gain_vector):
    widened = features.astype(jnp.float32)
    factor = lax.rsqrt(jnp.mean(widened * widened, axis=-1, keepdims=True) + norm_eps)
    return (widened * factor * gain_vector).astype(jnp.bfloat16)


def turned(head, cosines, sines):
    return (head * cosines + pltpu.roll(head, HD // 2, 1) * sines).astype(jnp.bfloat16)


def keys_values_kernel(normed, w_block, cosines, sines, out):
    block = jnp.dot(normed[...], w_block[...], preferred_element_type=jnp.float32)

    def write(columns, part):
        for copy in range(out.shape[0]):
            out[copy, :, columns] = part

    @pl.when(pl.program_id(0) == 0)
    def _():
        for k in range(KVH):
            columns = slice(k * HD, (k + 1) * HD)
            write(columns, turned(block[:, columns], cosines[...], sines[...]))

    @pl.when(pl.program_id(0) == 1)
    def _():
        write(slice(0, KVH * HD), block.astype(jnp.bfloat16))


def keys_values(normed, w_qkv, cosines, sines, copies):
    row_count, model_width = normed.shape
    width = KVH * HD
    whole = lambda i: (0, 0)
    return pl.pallas_call(
        keys_values_kernel,
        out_shape=jax.ShapeDtypeStruct((copies, row_count, 2 * width), jnp.bfloat16),
        grid=(2,),
        in_specs=[
            pl.BlockSpec((row_count, model_width), whole),
            pl.BlockSpec((model_width, width), lambda i: (0, QH * HD // width + i)),
            pl.BlockSpec((row_count, HD), whole),
            pl.BlockSpec((row_count, HD), whole),
        ],
        out_specs=pl.BlockSpec((copies, row_count, width), lambda i: (0, 0, i)),
        compiler_params=pltpu.CompilerParams(
            dimension_semantics=("arbitrary",), vmem_limit_bytes=32 << 20
        ),
    )(normed, w_qkv, cosines, sines)


def attention_kernel(projected, cosines, sines, kv_group, placing, start, place, out):
    allowed = (placing[...] >= start[...]) & (placing[...] <= place[...])
    share = QH // KVH
    for h in range(QH):
        columns = slice(h * HD, (h + 1) * HD)
        k = h // share
        query = turned(projected[:, columns], cosines[...], sines[...])
        scores = lax.dot_general(
            query,
            kv_group[:, k * HD : (k + 1) * HD],
            (((1,), (1,)), ((), ())),
            preferred_element_type=jnp.float32,
        ) * (HD ** (-0.5))
        scores = jnp.where(allowed, scores, masked_score)
        highest = jnp.max(scores, axis=1, keepdims=True)
        weights = jnp.where(allowed, jnp.exp(scores - highest), 0.0)
        denominator = jnp.sum(weights, axis=1, keepdims=True)
        numerator = jnp.dot(
            weights.astype(jnp.bfloat16),
            kv_group[:, (KVH + k) * HD : (KVH + k + 1) * HD],
            preferred_element_type=jnp.float32,
        )
        out[:, columns] = (numerator / denominator).astype(jnp.bfloat16)


def attention(projected, *operands):
    return pl.pallas_call(
        attention_kernel,
        out_shape=jax.ShapeDtypeStruct(projected.shape, jnp.bfloat16),
        compiler_params=pltpu.CompilerParams(vmem_limit_bytes=32 << 20),
    )(projected, *operands)


def spread(shard, axes, count):
    return lax.all_to_all(
        jnp.broadcast_to(shard[None], (count,) + shard.shape), axes, 0, 0, tiled=True
    )


CORES = [(0, 1), (1, 0)]
ROW_TILE = 256


def expert_kernel(rows, up, down, *rest):
    out = rest[-1]
    half_size = up.shape[1] // 2
    joined = jnp.dot(rows[...], up[...], preferred_element_type=jnp.float32)
    gate = joined[:, :half_size]
    active = (gate / (1.0 + jnp.exp(-gate)) * joined[:, half_size:]).astype(jnp.bfloat16)
    out[...] = jnp.dot(active, down[...], preferred_element_type=jnp.float32).astype(jnp.bfloat16)


def expert_half(rows, up, down, first, tiles, filled=None):
    kept = pl.BlockSpec(memory_space=pltpu.VMEM)
    tile = pl.BlockSpec((ROW_TILE, rows.shape[1]), lambda i: (first + i, 0))
    extra = [] if filled is None else [filled]
    return pl.pallas_call(
        expert_kernel,
        out_shape=jax.ShapeDtypeStruct(rows.shape, jnp.bfloat16),
        grid=(tiles,),
        in_specs=[tile, kept, kept] + [pl.BlockSpec(memory_space=pl.ANY)] * len(extra),
        out_specs=tile,
        input_output_aliases={} if filled is None else {3: 0},
        compiler_params=pltpu.CompilerParams(
            dimension_semantics=("arbitrary",), vmem_limit_bytes=40 << 20
        ),
        cost_estimate=pl.CostEstimate(
            flops=2 * tiles * ROW_TILE * (up.size + down.size),
            transcendentals=tiles * ROW_TILE * down.shape[0],
            bytes_accessed=4 * tiles * ROW_TILE * rows.shape[1],
        ),
    )(rows, up, down, *extra)


def per_device(
    hidden_in,
    placing,
    prompt_start,
    attn_gain,
    w_qkv,
    w_out,
    moe_gain,
    routes,
    route_weight,
    w_gate_up,
    w_down,
):
    row_count, model_width = hidden_in.shape
    query_width = QH * HD
    kv_width = KVH * HD
    my_index = lax.axis_index(CACHE)
    group_rows = placing.shape[0]
    cache_size = group_rows // row_count
    deal_rows = row_count // cache_size
    group_base = lax.axis_index(DP) * group_rows

    half_out = w_out.shape[1] // 2
    joint = jnp.concatenate(
        [w_qkv, jnp.concatenate([w_out[:, :half_out], w_out[:, half_out:]], axis=0)], axis=1
    )
    joint = spread(joint, CACHE, cache_size)
    qkv_rows = joint[:, :, : w_qkv.shape[1]].reshape(-1, w_qkv.shape[1])
    halves = joint[:, :, w_qkv.shape[1] :].reshape(cache_size, 2, w_out.shape[0], half_out)
    out_rows = jnp.concatenate([halves[:, 0], halves[:, 1]], axis=2).reshape(-1, w_out.shape[1])

    pairs = swap_pairs()
    sent_up, qkv_rows, out_rows = lax.optimization_barrier((w_gate_up[0], qkv_rows, out_rows))
    other_up = lax.ppermute(sent_up, ALL, pairs)
    keep = lax.axis_index("x") % 2 == lax.axis_index("core")

    full_qkv = lax.all_gather(qkv_rows, DP, axis=0, tiled=True)
    full_out = lax.all_gather(out_rows, DP, axis=0, tiled=True)
    full_qkv, other_up = lax.optimization_barrier((full_qkv, other_up))

    my_place = lax.dynamic_slice_in_dim(placing, my_index * row_count, row_count)
    position = my_place - prompt_start

    bits = routes
    chip_of = (
        (bits & 0b111000)
        | ((bits & 0b000011) << 1)
        | ((bits & 0b000100) >> 2)
    )
    named = chip_of[:, :, None] == jnp.arange(CHIP_COUNT, dtype=jnp.int32)[None, None, :]
    member = jnp.any(named, axis=1)
    weight_of = jnp.sum(jnp.where(named, route_weight[:, :, None], 0.0), axis=1)
    row_ids = jnp.arange(row_count, dtype=jnp.int32)
    before = (row_ids[:, None] > row_ids[None, :]).astype(jnp.bfloat16)
    rank = jnp.dot(before, member.astype(jnp.bfloat16), preferred_element_type=jnp.float32)
    rank = jnp.where(member, rank.astype(jnp.int32), -1).T
    chosen = rank[:, None, :] == jnp.arange(MOST, dtype=jnp.int32)[None, :, None]
    chosen = chosen.reshape(CHIP_COUNT * MOST, row_count)
    pick = chosen.astype(jnp.bfloat16)
    weighted = jnp.where(
        chosen.reshape(CHIP_COUNT, MOST, row_count), weight_of.T[:, None, :], 0.0
    ).reshape(CHIP_COUNT * MOST, row_count)
    weighted_hi = lax.reduce_precision(weighted, 8, 7)
    weighted_lo = (weighted - weighted_hi).astype(jnp.bfloat16)
    blend = jnp.concatenate([weighted_hi.astype(jnp.bfloat16), weighted_lo], axis=1)

    normed = rms_scaled(hidden_in, attn_gain)
    half_size = HD // 2
    inverse = rope_base ** (-(jnp.arange(half_size, dtype=jnp.float32) * 2.0 / HD))
    angles = position.astype(jnp.float32)[:, None] * inverse[None, :]
    cosine = jnp.cos(angles)
    sine_part = jnp.sin(angles)
    cosines = jnp.concatenate([cosine, cosine], axis=1)
    sines = jnp.concatenate([-sine_part, sine_part], axis=1)
    kv_copies = keys_values(normed, full_qkv, cosines, sines, cache_size)
    kv_group = lax.all_to_all(kv_copies, CACHE, 0, 0, tiled=True).reshape(group_rows, 2 * kv_width)
    projected = jnp.dot(normed, full_qkv[:, :query_width], preferred_element_type=jnp.float32)
    kv_group, projected, sent_down = lax.optimization_barrier((kv_group, projected, w_down[0]))
    other_down = lax.ppermute(sent_down, ALL, pairs)
    context = attention(
        projected, cosines, sines, kv_group, placing[None, :], prompt_start[:, None], my_place[:, None]
    )
    attn_out = jnp.dot(context, full_out, preferred_element_type=jnp.float32)
    attended = (hidden_in.astype(jnp.float32) + attn_out).astype(jnp.bfloat16)
    moe_in = rms_scaled(attended, moe_gain)

    outgoing = jnp.dot(pick, moe_in, preferred_element_type=jnp.float32).astype(jnp.bfloat16)
    outgoing, other_up, other_down = lax.optimization_barrier((outgoing, other_up, other_down))
    up = jnp.where(keep, w_gate_up[0], other_up)
    down = jnp.where(keep, w_down[0], other_down)
    mine = lax.all_to_all(
        outgoing.reshape(CHIP_COUNT, MOST, model_width), CHIPS, 0, 0, tiled=True
    ).reshape(CHIP_COUNT * MOST, model_width)
    mine, up, down = lax.optimization_barrier((mine, up, down))
    mates = lax.ppermute(mine, "core", CORES)
    tiles = mine.shape[0] // ROW_TILE
    own_part = expert_half(mine, up, down, 0, tiles // 2)
    mates, own_part = lax.optimization_barrier((mates, own_part))
    for_mate = expert_half(mates, up, down, 0, tiles)
    from_mate = lax.ppermute(for_mate, "core", CORES)
    own_part = expert_half(mine, up, down, tiles // 2, tiles // 2, own_part)
    expert_out = (own_part.astype(jnp.float32) + from_mate.astype(jnp.float32)).astype(jnp.bfloat16)
    returned = lax.all_to_all(
        expert_out.reshape(CHIP_COUNT, MOST, model_width), CHIPS, 0, 0, tiled=True
    ).reshape(CHIP_COUNT * MOST, model_width)
    blended = lax.dot_general(
        blend, returned, (((0,), (0,)), ((), ())), preferred_element_type=jnp.float32
    )
    mixture = blended[:row_count] + blended[row_count:]
    finished = (attended.astype(jnp.float32) + mixture).astype(jnp.bfloat16)

    home_rows = lax.all_to_all(
        finished.reshape(cache_size, deal_rows, model_width), CACHE, 0, 0, tiled=True
    ).reshape(row_count, model_width)
    my_base = group_base + my_index * row_count
    sender_place = lax.dynamic_slice_in_dim(
        placing.reshape(cache_size, row_count), my_index * deal_rows, deal_rows, axis=1
    ).reshape(-1)
    to_row = (sender_place[None, :] - my_base == row_ids[:, None]).astype(jnp.bfloat16)
    mixed = jnp.dot(to_row, home_rows, preferred_element_type=jnp.float32).astype(jnp.bfloat16)
    from_group = (placing[None, :] - my_base == row_ids[:, None]).astype(jnp.bfloat16)
    cached = jnp.dot(from_group, kv_group, preferred_element_type=jnp.float32).astype(jnp.bfloat16)
    return (mixed, cached[:, :kv_width], cached[:, kv_width:])


def solution(mesh):
    fine = Mesh(np.asarray(mesh.devices).reshape(tuple(SIZES[a] for a in ALL)), ALL)
    in_specs = (
        P(ALL, None),
        P(DP),
        P(ALL),
        P(),
        P(ALL, None),
        P(ALL, None),
        P(),
        P(ALL, None),
        P(ALL, None),
        P(ALL, None, None),
        P(ALL, None, None),
    )
    out_specs = (P(ALL, None), P(ALL, None), P(ALL, None))
    return jax.shard_map(
        per_device, mesh=fine, in_specs=in_specs, out_specs=out_specs, check_vma=False
    )
```

```python
import jax
import jax.numpy as jnp
import numpy as np
from jax import lax
from jax.experimental import pallas as pl
from jax.experimental.pallas import tpu as pltpu
from jax.sharding import Mesh
from jax.sharding import PartitionSpec as P

HD = 128
QH = 10
KVH = 2
TOP = 6
MOST = 16

DP = ("yh", "z", "core")
CACHE = ("yl", "x")
SIZES = {"yh": 2, "z": 4, "core": 2, "yl": 2, "x": 4}
ALL = DP + CACHE
CHIPS = ("yh", "z", "yl", "x")
CHIP_COUNT = 64

norm_eps = 1e-05
rope_base = 500000.0
masked_score = -1e30


def linear(yh, z, core, yl, x):
    return (((yh * 4 + z) * 2 + core) * 2 + yl) * 4 + x


def swap_pairs():
    pairs = []
    for yh in range(2):
        for z in range(4):
            for yl in range(2):
                for x in range(0, 4, 2):
                    low = linear(yh, z, 1, yl, x)
                    high = linear(yh, z, 0, yl, x + 1)
                    pairs += [(low, high), (high, low)]
    return pairs


def rms_scaled(features, gain_vector):
    widened = features.astype(jnp.float32)
    factor = lax.rsqrt(jnp.mean(widened * widened, axis=-1, keepdims=True) + norm_eps)
    return (widened * factor * gain_vector).astype(jnp.bfloat16)


def turned(head, cosines, sines):
    return (head * cosines + pltpu.roll(head, HD // 2, 1) * sines).astype(jnp.bfloat16)


def keys_values_kernel(projected, cosines, sines, out):
    for k in range(2 * KVH):
        columns = slice(k * HD, (k + 1) * HD)
        if k < KVH:
            part = turned(projected[:, columns], cosines[...], sines[...])
        else:
            part = projected[:, columns].astype(jnp.bfloat16)
        for device in range(out.shape[0]):
            out[device, :, columns] = part


def keys_values(projected, cosines, sines, copies):
    return pl.pallas_call(
        keys_values_kernel,
        out_shape=jax.ShapeDtypeStruct((copies,) + projected.shape, jnp.bfloat16),
    )(projected, cosines, sines)


def attention_kernel(projected, cosines, sines, kv_group, placing, start, place, out):
    allowed = (placing[...] >= start[...]) & (placing[...] <= place[...])
    share = QH // KVH
    for h in range(QH):
        columns = slice(h * HD, (h + 1) * HD)
        k = h // share
        query = turned(projected[:, columns], cosines[...], sines[...])
        scores = lax.dot_general(
            query,
            kv_group[:, k * HD : (k + 1) * HD],
            (((1,), (1,)), ((), ())),
            preferred_element_type=jnp.float32,
        ) * (HD ** (-0.5))
        scores = jnp.where(allowed, scores, masked_score)
        highest = jnp.max(scores, axis=1, keepdims=True)
        weights = jnp.where(allowed, jnp.exp(scores - highest), 0.0)
        denominator = jnp.sum(weights, axis=1, keepdims=True)
        numerator = jnp.dot(
            weights.astype(jnp.bfloat16),
            kv_group[:, (KVH + k) * HD : (KVH + k + 1) * HD],
            preferred_element_type=jnp.float32,
        )
        out[:, columns] = (numerator / denominator).astype(jnp.bfloat16)


def attention(projected, *operands):
    return pl.pallas_call(
        attention_kernel,
        out_shape=jax.ShapeDtypeStruct(projected.shape, jnp.bfloat16),
        compiler_params=pltpu.CompilerParams(vmem_limit_bytes=32 << 20),
    )(projected, *operands)


def spread(shard, axes, count):
    return lax.all_to_all(
        jnp.broadcast_to(shard[None], (count,) + shard.shape), axes, 0, 0, tiled=True
    )


CORES = [(0, 1), (1, 0)]
ROW_TILE = 256
UP_CHUNK = 640


def expert_kernel(keep, rows, own_up, other_up, own_down, other_first, other_second, *rest):
    out, up, down, up_sems, down_sems = rest[-5:]
    up_chunks = up.shape[0] // UP_CHUNK
    half_size = up.shape[1] // 2

    def up_copy(i, mine):
        part = pl.ds(i * UP_CHUNK, UP_CHUNK)
        source = own_up if mine else other_up
        return pltpu.make_async_copy(source.at[part], up.at[part], up_sems.at[i])

    down_half = down.shape[0] // 2

    def down_copy(i, mine):
        part = pl.ds(i * down_half, down_half)
        source = own_down.at[part] if mine else (other_first, other_second)[i]
        return pltpu.make_async_copy(source, down.at[part], down_sems.at[i])

    def finish(joined, wait):
        gate = joined[:, :half_size]
        active = (gate / (1.0 + jnp.exp(-gate)) * joined[:, half_size:]).astype(jnp.bfloat16)
        if wait:
            for i in range(2):
                down_copy(i, True).wait()
        out[...] = jnp.dot(active, down[...], preferred_element_type=jnp.float32).astype(jnp.bfloat16)

    @pl.when(pl.program_id(0) == 0)
    def _():
        @pl.when(keep[0] == 1)
        def _():
            for i in range(up_chunks):
                up_copy(i, True).start()
            for i in range(2):
                down_copy(i, True).start()

        @pl.when(keep[0] == 0)
        def _():
            for i in range(up_chunks):
                up_copy(i, False).start()
            for i in range(2):
                down_copy(i, False).start()

        joined = jnp.zeros((rows.shape[0], up.shape[1]), jnp.float32)
        for i in range(up_chunks):
            up_copy(i, True).wait()
            part = slice(i * UP_CHUNK, (i + 1) * UP_CHUNK)
            joined = joined + jnp.dot(
                rows[:, part], up[part, :], preferred_element_type=jnp.float32
            )
        finish(joined, True)

    @pl.when(pl.program_id(0) != 0)
    def _():
        finish(jnp.dot(rows[...], up[...], preferred_element_type=jnp.float32), False)


def expert_half(keep, rows, weights, first, tiles, filled=None):
    own_up, _, own_down, _, _ = weights
    anywhere = pl.BlockSpec(memory_space=pltpu.HBM)
    tile = pl.BlockSpec((ROW_TILE, rows.shape[1]), lambda i, keep: (first + i, 0))
    extra = [] if filled is None else [filled]
    return pl.pallas_call(
        expert_kernel,
        out_shape=jax.ShapeDtypeStruct(rows.shape, jnp.bfloat16),
        grid_spec=pltpu.PrefetchScalarGridSpec(
            num_scalar_prefetch=1,
            grid=(tiles,),
            in_specs=[tile] + [anywhere] * 5 + [pl.BlockSpec(memory_space=pl.ANY)] * len(extra),
            out_specs=tile,
            scratch_shapes=[
                pltpu.VMEM(own_up.shape, jnp.bfloat16),
                pltpu.VMEM(own_down.shape, jnp.bfloat16),
                pltpu.SemaphoreType.DMA((own_up.shape[0] // UP_CHUNK,)),
                pltpu.SemaphoreType.DMA((2,)),
            ],
        ),
        input_output_aliases={} if filled is None else {7: 0},
        compiler_params=pltpu.CompilerParams(
            dimension_semantics=("arbitrary",), vmem_limit_bytes=60 << 20
        ),
        cost_estimate=pl.CostEstimate(
            flops=2 * tiles * ROW_TILE * (own_up.size + own_down.size),
            transcendentals=tiles * ROW_TILE * own_down.shape[0],
            bytes_accessed=2 * (own_up.size + own_down.size)
            + 4 * tiles * ROW_TILE * rows.shape[1],
        ),
    )(keep, rows, *weights, *extra)


def per_device(
    hidden_in,
    placing,
    prompt_start,
    attn_gain,
    w_qkv,
    w_out,
    moe_gain,
    routes,
    route_weight,
    w_gate_up,
    w_down,
):
    row_count, model_width = hidden_in.shape
    query_width = QH * HD
    kv_width = KVH * HD
    my_index = lax.axis_index(CACHE)
    group_rows = placing.shape[0]
    cache_size = group_rows // row_count
    deal_rows = row_count // cache_size
    group_base = lax.axis_index(DP) * group_rows

    half_out = w_out.shape[1] // 2
    joint = jnp.concatenate(
        [w_qkv, jnp.concatenate([w_out[:, :half_out], w_out[:, half_out:]], axis=0)], axis=1
    )
    joint = spread(joint, CACHE, cache_size)
    qkv_rows = joint[:, :, : w_qkv.shape[1]].reshape(-1, w_qkv.shape[1])
    halves = joint[:, :, w_qkv.shape[1] :].reshape(cache_size, 2, w_out.shape[0], half_out)
    out_rows = jnp.concatenate([halves[:, 0], halves[:, 1]], axis=2).reshape(-1, w_out.shape[1])

    pairs = swap_pairs()
    down_half = w_down.shape[1] // 2
    sent_up, sent_first, qkv_rows, out_rows = lax.optimization_barrier(
        (w_gate_up[0], w_down[0, :down_half], qkv_rows, out_rows)
    )
    other_up = lax.ppermute(sent_up, ALL, pairs)
    other_first = lax.ppermute(sent_first, ALL, pairs)
    keep = lax.axis_index("x") % 2 == lax.axis_index("core")

    full_qkv = lax.all_gather(qkv_rows, DP, axis=0, tiled=True)
    full_out = lax.all_gather(out_rows, DP, axis=0, tiled=True)
    full_qkv, other_up = lax.optimization_barrier((full_qkv, other_up))

    my_place = lax.dynamic_slice_in_dim(placing, my_index * row_count, row_count)
    position = my_place - prompt_start

    bits = routes
    chip_of = (
        (bits & 0b111000)
        | ((bits & 0b000011) << 1)
        | ((bits & 0b000100) >> 2)
    )
    named = chip_of[:, :, None] == jnp.arange(CHIP_COUNT, dtype=jnp.int32)[None, None, :]
    member = jnp.any(named, axis=1)
    weight_of = jnp.sum(jnp.where(named, route_weight[:, :, None], 0.0), axis=1)
    row_ids = jnp.arange(row_count, dtype=jnp.int32)
    before = (row_ids[:, None] > row_ids[None, :]).astype(jnp.bfloat16)
    rank = jnp.dot(before, member.astype(jnp.bfloat16), preferred_element_type=jnp.float32)
    rank = jnp.where(member, rank.astype(jnp.int32), -1).T
    chosen = rank[:, None, :] == jnp.arange(MOST, dtype=jnp.int32)[None, :, None]
    chosen = chosen.reshape(CHIP_COUNT * MOST, row_count)
    pick = chosen.astype(jnp.bfloat16)
    weighted = jnp.where(
        chosen.reshape(CHIP_COUNT, MOST, row_count), weight_of.T[:, None, :], 0.0
    ).reshape(CHIP_COUNT * MOST, row_count)
    weighted_hi = lax.reduce_precision(weighted, 8, 7)
    weighted_lo = (weighted - weighted_hi).astype(jnp.bfloat16)
    blend = jnp.concatenate([weighted_hi.astype(jnp.bfloat16), weighted_lo], axis=1)

    normed = rms_scaled(hidden_in, attn_gain)
    half_size = HD // 2
    inverse = rope_base ** (-(jnp.arange(half_size, dtype=jnp.float32) * 2.0 / HD))
    angles = position.astype(jnp.float32)[:, None] * inverse[None, :]
    cosine = jnp.cos(angles)
    sine_part = jnp.sin(angles)
    cosines = jnp.concatenate([cosine, cosine], axis=1)
    sines = jnp.concatenate([-sine_part, sine_part], axis=1)
    kv_projected = jnp.dot(normed, full_qkv[:, query_width:], preferred_element_type=jnp.float32)
    kv_copies = keys_values(kv_projected, cosines, sines, cache_size)
    kv_group = lax.all_to_all(kv_copies, CACHE, 0, 0, tiled=True).reshape(group_rows, 2 * kv_width)
    projected = jnp.dot(normed, full_qkv[:, :query_width], preferred_element_type=jnp.float32)
    kv_group, projected, other_first, sent_second = lax.optimization_barrier(
        (kv_group, projected, other_first, w_down[0, down_half:])
    )
    other_second = lax.ppermute(sent_second, ALL, pairs)
    context = attention(
        projected, cosines, sines, kv_group, placing[None, :], prompt_start[:, None], my_place[:, None]
    )
    attn_out = jnp.dot(context, full_out, preferred_element_type=jnp.float32)
    attended = (hidden_in.astype(jnp.float32) + attn_out).astype(jnp.bfloat16)
    moe_in = rms_scaled(attended, moe_gain)

    outgoing = jnp.dot(pick, moe_in, preferred_element_type=jnp.float32).astype(jnp.bfloat16)
    outgoing, other_second = lax.optimization_barrier((outgoing, other_second))
    mine = lax.all_to_all(
        outgoing.reshape(CHIP_COUNT, MOST, model_width), CHIPS, 0, 0, tiled=True
    ).reshape(CHIP_COUNT * MOST, model_width)
    mates = lax.ppermute(mine, "core", CORES)
    weights = (w_gate_up[0], other_up, w_down[0], other_first, other_second)
    kept = keep.astype(jnp.int32).reshape(1)
    tiles = mine.shape[0] // ROW_TILE
    own_part = expert_half(kept, mine, weights, 0, tiles // 2)
    mates, own_part = lax.optimization_barrier((mates, own_part))
    for_mate = expert_half(kept, mates, weights, 0, tiles)
    from_mate = lax.ppermute(for_mate, "core", CORES)
    own_part = expert_half(kept, mine, weights, tiles // 2, tiles // 2, own_part)
    expert_out = (own_part.astype(jnp.float32) + from_mate.astype(jnp.float32)).astype(jnp.bfloat16)
    returned = lax.all_to_all(
        expert_out.reshape(CHIP_COUNT, MOST, model_width), CHIPS, 0, 0, tiled=True
    ).reshape(CHIP_COUNT * MOST, model_width)
    blended = lax.dot_general(
        blend, returned, (((0,), (0,)), ((), ())), preferred_element_type=jnp.float32
    )
    mixture = blended[:row_count] + blended[row_count:]
    finished = (attended.astype(jnp.float32) + mixture).astype(jnp.bfloat16)

    home_rows = lax.all_to_all(
        finished.reshape(cache_size, deal_rows, model_width), CACHE, 0, 0, tiled=True
    ).reshape(row_count, model_width)
    my_base = group_base + my_index * row_count
    sender_place = lax.dynamic_slice_in_dim(
        placing.reshape(cache_size, row_count), my_index * deal_rows, deal_rows, axis=1
    ).reshape(-1)
    to_row = (sender_place[None, :] - my_base == row_ids[:, None]).astype(jnp.bfloat16)
    mixed = jnp.dot(to_row, home_rows, preferred_element_type=jnp.float32).astype(jnp.bfloat16)
    from_group = (placing[None, :] - my_base == row_ids[:, None]).astype(jnp.bfloat16)
    cached = jnp.dot(from_group, kv_group, preferred_element_type=jnp.float32).astype(jnp.bfloat16)
    return (mixed, cached[:, :kv_width], cached[:, kv_width:])


def solution(mesh):
    fine = Mesh(np.asarray(mesh.devices).reshape(tuple(SIZES[a] for a in ALL)), ALL)
    in_specs = (
        P(ALL, None),
        P(DP),
        P(ALL),
        P(),
        P(ALL, None),
        P(ALL, None),
        P(),
        P(ALL, None),
        P(ALL, None),
        P(ALL, None, None),
        P(ALL, None, None),
    )
    out_specs = (P(ALL, None), P(ALL, None), P(ALL, None))
    return jax.shard_map(
        per_device, mesh=fine, in_specs=in_specs, out_specs=out_specs, check_vma=False
    )
```

```python
import jax
import jax.numpy as jnp
import numpy as np
from jax import lax
from jax.experimental import pallas as pl
from jax.experimental.pallas import tpu as pltpu
from jax.sharding import Mesh
from jax.sharding import PartitionSpec as P

HD = 128
QH = 10
KVH = 2
TOP = 6
MOST = 16

DP = ("yh", "z", "core")
CACHE = ("yl", "x")
SIZES = {"yh": 2, "z": 4, "core": 2, "yl": 2, "x": 4}
ALL = DP + CACHE
CHIPS = ("yh", "z", "yl", "x")
CHIP_COUNT = 64

norm_eps = 1e-05
rope_base = 500000.0
masked_score = -1e30


def linear(yh, z, core, yl, x):
    return (((yh * 4 + z) * 2 + core) * 2 + yl) * 4 + x


def swap_pairs():
    pairs = []
    for yh in range(2):
        for z in range(4):
            for yl in range(2):
                for x in range(0, 4, 2):
                    low = linear(yh, z, 1, yl, x)
                    high = linear(yh, z, 0, yl, x + 1)
                    pairs += [(low, high), (high, low)]
    return pairs


def rms_scaled(features, gain_vector):
    widened = features.astype(jnp.float32)
    factor = lax.rsqrt(jnp.mean(widened * widened, axis=-1, keepdims=True) + norm_eps)
    return (widened * factor * gain_vector).astype(jnp.bfloat16)


def turned(head, cosines, sines):
    return (head * cosines + pltpu.roll(head, HD // 2, 1) * sines).astype(jnp.bfloat16)


def keys_values_kernel(projected, cosines, sines, out):
    for k in range(2 * KVH):
        columns = slice(k * HD, (k + 1) * HD)
        if k < KVH:
            part = turned(projected[:, columns], cosines[...], sines[...])
        else:
            part = projected[:, columns].astype(jnp.bfloat16)
        for device in range(out.shape[0]):
            out[device, :, columns] = part


def keys_values(projected, cosines, sines, copies):
    return pl.pallas_call(
        keys_values_kernel,
        out_shape=jax.ShapeDtypeStruct((copies,) + projected.shape, jnp.bfloat16),
    )(projected, cosines, sines)


def attention_kernel(projected, cosines, sines, kv_group, placing, start, place, out):
    allowed = (placing[...] >= start[...]) & (placing[...] <= place[...])
    share = QH // KVH
    for h in range(QH):
        columns = slice(h * HD, (h + 1) * HD)
        k = h // share
        query = turned(projected[:, columns], cosines[...], sines[...])
        scores = lax.dot_general(
            query,
            kv_group[:, k * HD : (k + 1) * HD],
            (((1,), (1,)), ((), ())),
            preferred_element_type=jnp.float32,
        ) * (HD ** (-0.5))
        scores = jnp.where(allowed, scores, masked_score)
        highest = jnp.max(scores, axis=1, keepdims=True)
        weights = jnp.where(allowed, jnp.exp(scores - highest), 0.0)
        denominator = jnp.sum(weights, axis=1, keepdims=True)
        numerator = jnp.dot(
            weights.astype(jnp.bfloat16),
            kv_group[:, (KVH + k) * HD : (KVH + k + 1) * HD],
            preferred_element_type=jnp.float32,
        )
        out[:, columns] = (numerator / denominator).astype(jnp.bfloat16)


def attention(projected, *operands):
    return pl.pallas_call(
        attention_kernel,
        out_shape=jax.ShapeDtypeStruct(projected.shape, jnp.bfloat16),
        compiler_params=pltpu.CompilerParams(vmem_limit_bytes=32 << 20),
    )(projected, *operands)


def spread(shard, axes, count):
    return lax.all_to_all(
        jnp.broadcast_to(shard[None], (count,) + shard.shape), axes, 0, 0, tiled=True
    )


CORES = [(0, 1), (1, 0)]
ROW_TILE = 256
UP_CHUNK = 640


def expert_kernel(keep, rows, own_up, other_up, own_down, other_first, other_second, *rest):
    out, up, down, up_sems, down_sems = rest[-5:]
    up_chunks = up.shape[0] // UP_CHUNK
    half_size = up.shape[1] // 2

    def up_copy(i, mine):
        part = pl.ds(i * UP_CHUNK, UP_CHUNK)
        source = own_up if mine else other_up
        return pltpu.make_async_copy(source.at[part], up.at[part], up_sems.at[i])

    down_half = down.shape[0] // 2

    def down_copy(i, mine):
        part = pl.ds(i * down_half, down_half)
        source = own_down.at[part] if mine else (other_first, other_second)[i]
        return pltpu.make_async_copy(source, down.at[part], down_sems.at[i])

    def finish(joined, wait):
        gate = joined[:, :half_size]
        active = (gate / (1.0 + jnp.exp(-gate)) * joined[:, half_size:]).astype(jnp.bfloat16)
        if wait:
            for i in range(2):
                down_copy(i, True).wait()
        out[...] = jnp.dot(active, down[...], preferred_element_type=jnp.float32).astype(jnp.bfloat16)

    @pl.when(pl.program_id(0) == 0)
    def _():
        @pl.when(keep[0] == 1)
        def _():
            for i in range(up_chunks):
                up_copy(i, True).start()
            for i in range(2):
                down_copy(i, True).start()

        @pl.when(keep[0] == 0)
        def _():
            for i in range(up_chunks):
                up_copy(i, False).start()
            for i in range(2):
                down_copy(i, False).start()

        joined = jnp.zeros((rows.shape[0], up.shape[1]), jnp.float32)
        for i in range(up_chunks):
            up_copy(i, True).wait()
            part = slice(i * UP_CHUNK, (i + 1) * UP_CHUNK)
            joined = joined + jnp.dot(
                rows[:, part], up[part, :], preferred_element_type=jnp.float32
            )
        finish(joined, True)

    @pl.when(pl.program_id(0) != 0)
    def _():
        finish(jnp.dot(rows[...], up[...], preferred_element_type=jnp.float32), False)


def expert_half(keep, rows, weights, first, tiles, filled=None):
    own_up, _, own_down, _, _ = weights
    anywhere = pl.BlockSpec(memory_space=pltpu.HBM)
    tile = pl.BlockSpec((ROW_TILE, rows.shape[1]), lambda i, keep: (first + i, 0))
    extra = [] if filled is None else [filled]
    return pl.pallas_call(
        expert_kernel,
        out_shape=jax.ShapeDtypeStruct(rows.shape, jnp.bfloat16),
        grid_spec=pltpu.PrefetchScalarGridSpec(
            num_scalar_prefetch=1,
            grid=(tiles,),
            in_specs=[tile] + [anywhere] * 5 + [pl.BlockSpec(memory_space=pl.ANY)] * len(extra),
            out_specs=tile,
            scratch_shapes=[
                pltpu.VMEM(own_up.shape, jnp.bfloat16),
                pltpu.VMEM(own_down.shape, jnp.bfloat16),
                pltpu.SemaphoreType.DMA((own_up.shape[0] // UP_CHUNK,)),
                pltpu.SemaphoreType.DMA((2,)),
            ],
        ),
        input_output_aliases={} if filled is None else {7: 0},
        compiler_params=pltpu.CompilerParams(
            dimension_semantics=("arbitrary",), vmem_limit_bytes=60 << 20
        ),
        cost_estimate=pl.CostEstimate(
            flops=2 * tiles * ROW_TILE * (own_up.size + own_down.size),
            transcendentals=tiles * ROW_TILE * own_down.shape[0],
            bytes_accessed=2 * (own_up.size + own_down.size)
            + 4 * tiles * ROW_TILE * rows.shape[1],
        ),
    )(keep, rows, *weights, *extra)


def per_device(
    hidden_in,
    placing,
    prompt_start,
    attn_gain,
    w_qkv,
    w_out,
    moe_gain,
    routes,
    route_weight,
    w_gate_up,
    w_down,
):
    row_count, model_width = hidden_in.shape
    query_width = QH * HD
    kv_width = KVH * HD
    my_index = lax.axis_index(CACHE)
    group_rows = placing.shape[0]
    cache_size = group_rows // row_count
    deal_rows = row_count // cache_size
    group_base = lax.axis_index(DP) * group_rows

    half_out = w_out.shape[1] // 2
    joint = jnp.concatenate(
        [w_qkv, jnp.concatenate([w_out[:, :half_out], w_out[:, half_out:]], axis=0)], axis=1
    )
    joint = spread(joint, CACHE, cache_size)
    qkv_rows = joint[:, :, : w_qkv.shape[1]].reshape(-1, w_qkv.shape[1])
    halves = joint[:, :, w_qkv.shape[1] :].reshape(cache_size, 2, w_out.shape[0], half_out)
    out_rows = jnp.concatenate([halves[:, 0], halves[:, 1]], axis=2).reshape(-1, w_out.shape[1])

    pairs = swap_pairs()
    down_half = w_down.shape[1] // 2
    sent_up, sent_first, qkv_rows, out_rows = lax.optimization_barrier(
        (w_gate_up[0], w_down[0, :down_half], qkv_rows, out_rows)
    )
    other_up = lax.ppermute(sent_up, ALL, pairs)
    other_first = lax.ppermute(sent_first, ALL, pairs)
    keep = lax.axis_index("x") % 2 == lax.axis_index("core")

    out_halves = jnp.concatenate([out_rows[:, :half_out], out_rows[:, half_out:]], axis=0)
    gathered = lax.all_gather(
        jnp.concatenate([qkv_rows, out_halves], axis=1), DP, axis=0, tiled=True
    )
    gathered, other_up = lax.optimization_barrier((gathered, other_up))
    full_qkv = gathered[:, : w_qkv.shape[1]]
    out_parts = gathered[:, w_qkv.shape[1] :].reshape(-1, 2, out_rows.shape[0], half_out)
    out_left = out_parts[:, 0].reshape(-1, half_out)
    out_right = out_parts[:, 1].reshape(-1, half_out)

    my_place = lax.dynamic_slice_in_dim(placing, my_index * row_count, row_count)
    position = my_place - prompt_start

    bits = routes
    chip_of = (
        (bits & 0b111000)
        | ((bits & 0b000011) << 1)
        | ((bits & 0b000100) >> 2)
    )
    named = chip_of[:, :, None] == jnp.arange(CHIP_COUNT, dtype=jnp.int32)[None, None, :]
    member = jnp.any(named, axis=1)
    weight_of = jnp.sum(jnp.where(named, route_weight[:, :, None], 0.0), axis=1)
    row_ids = jnp.arange(row_count, dtype=jnp.int32)
    before = (row_ids[:, None] > row_ids[None, :]).astype(jnp.bfloat16)
    rank = jnp.dot(before, member.astype(jnp.bfloat16), preferred_element_type=jnp.float32)
    rank = jnp.where(member, rank.astype(jnp.int32), -1).T
    chosen = rank[:, None, :] == jnp.arange(MOST, dtype=jnp.int32)[None, :, None]
    chosen = chosen.reshape(CHIP_COUNT * MOST, row_count)
    pick = chosen.astype(jnp.bfloat16)
    weighted = jnp.where(
        chosen.reshape(CHIP_COUNT, MOST, row_count), weight_of.T[:, None, :], 0.0
    ).reshape(CHIP_COUNT * MOST, row_count)
    weighted_hi = lax.reduce_precision(weighted, 8, 7)
    weighted_lo = (weighted - weighted_hi).astype(jnp.bfloat16)
    blend = jnp.concatenate([weighted_hi.astype(jnp.bfloat16), weighted_lo], axis=1)
    blend = lax.optimization_barrier(blend.T)

    normed = rms_scaled(hidden_in, attn_gain)
    half_size = HD // 2
    inverse = rope_base ** (-(jnp.arange(half_size, dtype=jnp.float32) * 2.0 / HD))
    angles = position.astype(jnp.float32)[:, None] * inverse[None, :]
    cosine = jnp.cos(angles)
    sine_part = jnp.sin(angles)
    cosines = jnp.concatenate([cosine, cosine], axis=1)
    sines = jnp.concatenate([-sine_part, sine_part], axis=1)
    kv_projected = jnp.dot(normed, full_qkv[:, query_width:], preferred_element_type=jnp.float32)
    kv_copies = keys_values(kv_projected, cosines, sines, cache_size)
    kv_group = lax.all_to_all(kv_copies, CACHE, 0, 0, tiled=True).reshape(group_rows, 2 * kv_width)
    projected = jnp.dot(normed, full_qkv[:, :query_width], preferred_element_type=jnp.float32)
    kv_group, projected, out_left, out_right, other_first, sent_second = lax.optimization_barrier(
        (kv_group, projected, out_left, out_right, other_first, w_down[0, down_half:])
    )
    other_second = lax.ppermute(sent_second, ALL, pairs)
    context = attention(
        projected, cosines, sines, kv_group, placing[None, :], prompt_start[:, None], my_place[:, None]
    )
    attn_out = jnp.concatenate(
        [
            jnp.dot(context, part, preferred_element_type=jnp.float32)
            for part in (out_left, out_right)
        ],
        axis=1,
    )
    attended = (hidden_in.astype(jnp.float32) + attn_out).astype(jnp.bfloat16)
    moe_in = rms_scaled(attended, moe_gain)

    outgoing = jnp.dot(pick, moe_in, preferred_element_type=jnp.float32).astype(jnp.bfloat16)
    outgoing, other_second = lax.optimization_barrier((outgoing, other_second))
    mine = lax.all_to_all(
        outgoing.reshape(CHIP_COUNT, MOST, model_width), CHIPS, 0, 0, tiled=True
    ).reshape(CHIP_COUNT * MOST, model_width)
    mates = lax.ppermute(mine, "core", CORES)
    weights = (w_gate_up[0], other_up, w_down[0], other_first, other_second)
    kept = keep.astype(jnp.int32).reshape(1)
    tiles = mine.shape[0] // ROW_TILE
    own_part = expert_half(kept, mine, weights, 0, tiles // 2)
    mates, own_part = lax.optimization_barrier((mates, own_part))
    for_mate = expert_half(kept, mates, weights, 0, tiles)
    from_mate = lax.ppermute(for_mate, "core", CORES)
    own_part = expert_half(kept, mine, weights, tiles // 2, tiles // 2, own_part)
    expert_out = (own_part.astype(jnp.float32) + from_mate.astype(jnp.float32)).astype(jnp.bfloat16)
    returned = lax.all_to_all(
        expert_out.reshape(CHIP_COUNT, MOST, model_width), CHIPS, 0, 0, tiled=True
    ).reshape(CHIP_COUNT * MOST, model_width)
    blended = jnp.dot(blend, returned, preferred_element_type=jnp.float32)
    mixture = blended[:row_count] + blended[row_count:]
    finished = (attended.astype(jnp.float32) + mixture).astype(jnp.bfloat16)

    home_rows = lax.all_to_all(
        finished.reshape(cache_size, deal_rows, model_width), CACHE, 0, 0, tiled=True
    ).reshape(row_count, model_width)
    my_base = group_base + my_index * row_count
    sender_place = lax.dynamic_slice_in_dim(
        placing.reshape(cache_size, row_count), my_index * deal_rows, deal_rows, axis=1
    ).reshape(-1)
    to_row = (sender_place[None, :] - my_base == row_ids[:, None]).astype(jnp.bfloat16)
    mixed = jnp.dot(to_row, home_rows, preferred_element_type=jnp.float32).astype(jnp.bfloat16)
    from_group = (placing[None, :] - my_base == row_ids[:, None]).astype(jnp.bfloat16)
    cached = jnp.dot(from_group, kv_group, preferred_element_type=jnp.float32).astype(jnp.bfloat16)
    return (mixed, cached[:, :kv_width], cached[:, kv_width:])


def solution(mesh):
    fine = Mesh(np.asarray(mesh.devices).reshape(tuple(SIZES[a] for a in ALL)), ALL)
    in_specs = (
        P(ALL, None),
        P(DP),
        P(ALL),
        P(),
        P(ALL, None),
        P(ALL, None),
        P(),
        P(ALL, None),
        P(ALL, None),
        P(ALL, None, None),
        P(ALL, None, None),
    )
    out_specs = (P(ALL, None), P(ALL, None), P(ALL, None))
    return jax.shard_map(
        per_device, mesh=fine, in_specs=in_specs, out_specs=out_specs, check_vma=False
    )
```

```python
import jax
import jax.numpy as jnp
import numpy as np
from jax import lax
from jax.experimental import pallas as pl
from jax.experimental.pallas import tpu as pltpu
from jax.sharding import Mesh
from jax.sharding import PartitionSpec as P

HD = 128
QH = 10
KVH = 2
TOP = 6
MOST = 16

DP = ("yh", "z", "core")
CACHE = ("yl", "x")
SIZES = {"yh": 2, "z": 4, "core": 2, "yl": 2, "x": 4}
ALL = DP + CACHE
CHIPS = ("yh", "z", "yl", "x")
CHIP_COUNT = 64

norm_eps = 1e-05
rope_base = 500000.0
masked_score = -1e30


def linear(yh, z, core, yl, x):
    return (((yh * 4 + z) * 2 + core) * 2 + yl) * 4 + x


def swap_pairs():
    pairs = []
    for yh in range(2):
        for z in range(4):
            for yl in range(2):
                for x in range(0, 4, 2):
                    low = linear(yh, z, 1, yl, x)
                    high = linear(yh, z, 0, yl, x + 1)
                    pairs += [(low, high), (high, low)]
    return pairs


def rms_scaled(features, gain_vector):
    widened = features.astype(jnp.float32)
    factor = lax.rsqrt(jnp.mean(widened * widened, axis=-1, keepdims=True) + norm_eps)
    return (widened * factor * gain_vector).astype(jnp.bfloat16)


def turned(head, cosines, sines):
    return (head * cosines + pltpu.roll(head, HD // 2, 1) * sines).astype(jnp.bfloat16)


def keys_values_kernel(projected, cosines, sines, out):
    for k in range(2 * KVH):
        columns = slice(k * HD, (k + 1) * HD)
        if k < KVH:
            part = turned(projected[:, columns], cosines[...], sines[...])
        else:
            part = projected[:, columns].astype(jnp.bfloat16)
        for device in range(out.shape[0]):
            out[device, :, columns] = part


def keys_values(projected, cosines, sines, copies):
    return pl.pallas_call(
        keys_values_kernel,
        out_shape=jax.ShapeDtypeStruct((copies,) + projected.shape, jnp.bfloat16),
    )(projected, cosines, sines)


def attention_kernel(projected, cosines, sines, kv_group, placing, start, place, out):
    allowed = (placing[...] >= start[...]) & (placing[...] <= place[...])
    share = QH // KVH
    for h in range(QH):
        columns = slice(h * HD, (h + 1) * HD)
        k = h // share
        query = turned(projected[:, columns], cosines[...], sines[...])
        scores = lax.dot_general(
            query,
            kv_group[:, k * HD : (k + 1) * HD],
            (((1,), (1,)), ((), ())),
            preferred_element_type=jnp.float32,
        ) * (HD ** (-0.5))
        scores = jnp.where(allowed, scores, masked_score)
        highest = jnp.max(scores, axis=1, keepdims=True)
        weights = jnp.where(allowed, jnp.exp(scores - highest), 0.0)
        denominator = jnp.sum(weights, axis=1, keepdims=True)
        numerator = jnp.dot(
            weights.astype(jnp.bfloat16),
            kv_group[:, (KVH + k) * HD : (KVH + k + 1) * HD],
            preferred_element_type=jnp.float32,
        )
        out[:, columns] = (numerator / denominator).astype(jnp.bfloat16)


def attention(projected, *operands):
    return pl.pallas_call(
        attention_kernel,
        out_shape=jax.ShapeDtypeStruct(projected.shape, jnp.bfloat16),
        compiler_params=pltpu.CompilerParams(vmem_limit_bytes=32 << 20),
    )(projected, *operands)


def spread(shard, axes, count):
    return lax.all_to_all(
        jnp.broadcast_to(shard[None], (count,) + shard.shape), axes, 0, 0, tiled=True
    )


CORES = [(0, 1), (1, 0)]
ROW_TILE = 256
UP_CHUNK = 640


def expert_kernel(keep, rows, own_up, other_up, own_down, other_first, other_second, *rest):
    out, up, down, up_sems, down_sems = rest[-5:]
    up_chunks = up.shape[0] // UP_CHUNK
    half_size = up.shape[1] // 2

    def up_copy(i, mine):
        part = pl.ds(i * UP_CHUNK, UP_CHUNK)
        source = own_up if mine else other_up
        return pltpu.make_async_copy(source.at[part], up.at[part], up_sems.at[i])

    first_rows = other_first.shape[0]

    def down_copy(i, mine):
        part = (pl.ds(0, first_rows), pl.ds(first_rows, down.shape[0] - first_rows))[i]
        source = own_down.at[part] if mine else (other_first, other_second)[i]
        return pltpu.make_async_copy(source, down.at[part], down_sems.at[i])

    def finish(joined, wait):
        gate = joined[:, :half_size]
        active = (gate / (1.0 + jnp.exp(-gate)) * joined[:, half_size:]).astype(jnp.bfloat16)
        if wait:
            for i in range(2):
                down_copy(i, True).wait()
        out[...] = jnp.dot(active, down[...], preferred_element_type=jnp.float32).astype(jnp.bfloat16)

    @pl.when(pl.program_id(0) == 0)
    def _():
        @pl.when(keep[0] == 1)
        def _():
            for i in range(up_chunks):
                up_copy(i, True).start()
            for i in range(2):
                down_copy(i, True).start()

        @pl.when(keep[0] == 0)
        def _():
            for i in range(up_chunks):
                up_copy(i, False).start()
            for i in range(2):
                down_copy(i, False).start()

        joined = jnp.zeros((rows.shape[0], up.shape[1]), jnp.float32)
        for i in range(up_chunks):
            up_copy(i, True).wait()
            part = slice(i * UP_CHUNK, (i + 1) * UP_CHUNK)
            joined = joined + jnp.dot(
                rows[:, part], up[part, :], preferred_element_type=jnp.float32
            )
        finish(joined, True)

    @pl.when(pl.program_id(0) != 0)
    def _():
        finish(jnp.dot(rows[...], up[...], preferred_element_type=jnp.float32), False)


def expert_half(keep, rows, weights, first, tiles, filled=None):
    own_up, _, own_down, _, _ = weights
    anywhere = pl.BlockSpec(memory_space=pltpu.HBM)
    tile = pl.BlockSpec((ROW_TILE, rows.shape[1]), lambda i, keep: (first + i, 0))
    extra = [] if filled is None else [filled]
    return pl.pallas_call(
        expert_kernel,
        out_shape=jax.ShapeDtypeStruct(rows.shape, jnp.bfloat16),
        grid_spec=pltpu.PrefetchScalarGridSpec(
            num_scalar_prefetch=1,
            grid=(tiles,),
            in_specs=[tile] + [anywhere] * 5 + [pl.BlockSpec(memory_space=pl.ANY)] * len(extra),
            out_specs=tile,
            scratch_shapes=[
                pltpu.VMEM(own_up.shape, jnp.bfloat16),
                pltpu.VMEM(own_down.shape, jnp.bfloat16),
                pltpu.SemaphoreType.DMA((own_up.shape[0] // UP_CHUNK,)),
                pltpu.SemaphoreType.DMA((2,)),
            ],
        ),
        input_output_aliases={} if filled is None else {7: 0},
        compiler_params=pltpu.CompilerParams(
            dimension_semantics=("arbitrary",), vmem_limit_bytes=60 << 20
        ),
        cost_estimate=pl.CostEstimate(
            flops=2 * tiles * ROW_TILE * (own_up.size + own_down.size),
            transcendentals=tiles * ROW_TILE * own_down.shape[0],
            bytes_accessed=2 * (own_up.size + own_down.size)
            + 4 * tiles * ROW_TILE * rows.shape[1],
        ),
    )(keep, rows, *weights, *extra)


def per_device(
    hidden_in,
    placing,
    prompt_start,
    attn_gain,
    w_qkv,
    w_out,
    moe_gain,
    routes,
    route_weight,
    w_gate_up,
    w_down,
):
    row_count, model_width = hidden_in.shape
    query_width = QH * HD
    kv_width = KVH * HD
    my_index = lax.axis_index(CACHE)
    group_rows = placing.shape[0]
    cache_size = group_rows // row_count
    deal_rows = row_count // cache_size
    group_base = lax.axis_index(DP) * group_rows

    half_out = w_out.shape[1] // 2
    joint = jnp.concatenate(
        [w_qkv, jnp.concatenate([w_out[:, :half_out], w_out[:, half_out:]], axis=0)], axis=1
    )
    joint = spread(joint, CACHE, cache_size)
    qkv_rows = joint[:, :, : w_qkv.shape[1]].reshape(-1, w_qkv.shape[1])
    halves = joint[:, :, w_qkv.shape[1] :].reshape(cache_size, 2, w_out.shape[0], half_out)
    out_rows = jnp.concatenate([halves[:, 0], halves[:, 1]], axis=2).reshape(-1, w_out.shape[1])

    pairs = swap_pairs()
    first_rows = w_down.shape[1] * 3 // 4
    sent_up, sent_first, qkv_rows, out_rows = lax.optimization_barrier(
        (w_gate_up[0], w_down[0, :first_rows], qkv_rows, out_rows)
    )
    other_up = lax.ppermute(sent_up, ALL, pairs)
    other_first = lax.ppermute(sent_first, ALL, pairs)
    keep = lax.axis_index("x") % 2 == lax.axis_index("core")

    out_halves = jnp.concatenate([out_rows[:, :half_out], out_rows[:, half_out:]], axis=0)
    gathered = lax.all_gather(
        jnp.concatenate([qkv_rows, out_halves], axis=1), DP, axis=0, tiled=True
    )
    gathered, other_up = lax.optimization_barrier((gathered, other_up))
    full_qkv = gathered[:, : w_qkv.shape[1]]
    out_parts = gathered[:, w_qkv.shape[1] :].reshape(-1, 2, out_rows.shape[0], half_out)
    out_left = out_parts[:, 0].reshape(-1, half_out)
    out_right = out_parts[:, 1].reshape(-1, half_out)

    my_place = lax.dynamic_slice_in_dim(placing, my_index * row_count, row_count)
    position = my_place - prompt_start

    bits = routes
    chip_of = (
        (bits & 0b111000)
        | ((bits & 0b000011) << 1)
        | ((bits & 0b000100) >> 2)
    )
    named = chip_of[:, :, None] == jnp.arange(CHIP_COUNT, dtype=jnp.int32)[None, None, :]
    member = jnp.any(named, axis=1)
    weight_of = jnp.sum(jnp.where(named, route_weight[:, :, None], 0.0), axis=1)
    row_ids = jnp.arange(row_count, dtype=jnp.int32)
    before = (row_ids[:, None] > row_ids[None, :]).astype(jnp.bfloat16)
    rank = jnp.dot(before, member.astype(jnp.bfloat16), preferred_element_type=jnp.float32)
    rank = jnp.where(member, rank.astype(jnp.int32), -1).T
    chosen = rank[:, None, :] == jnp.arange(MOST, dtype=jnp.int32)[None, :, None]
    chosen = chosen.reshape(CHIP_COUNT * MOST, row_count)
    pick = chosen.astype(jnp.bfloat16)
    weighted = jnp.where(
        chosen.reshape(CHIP_COUNT, MOST, row_count), weight_of.T[:, None, :], 0.0
    ).reshape(CHIP_COUNT * MOST, row_count)
    weighted_hi = lax.reduce_precision(weighted, 8, 7)
    weighted_lo = (weighted - weighted_hi).astype(jnp.bfloat16)
    blend = jnp.concatenate([weighted_hi.astype(jnp.bfloat16), weighted_lo], axis=1)
    blend = lax.optimization_barrier(blend.T)

    normed = rms_scaled(hidden_in, attn_gain)
    half_size = HD // 2
    inverse = rope_base ** (-(jnp.arange(half_size, dtype=jnp.float32) * 2.0 / HD))
    angles = position.astype(jnp.float32)[:, None] * inverse[None, :]
    cosine = jnp.cos(angles)
    sine_part = jnp.sin(angles)
    cosines = jnp.concatenate([cosine, cosine], axis=1)
    sines = jnp.concatenate([-sine_part, sine_part], axis=1)
    kv_projected = jnp.dot(normed, full_qkv[:, query_width:], preferred_element_type=jnp.float32)
    kv_copies = keys_values(kv_projected, cosines, sines, cache_size)
    kv_group = lax.all_to_all(kv_copies, CACHE, 0, 0, tiled=True).reshape(group_rows, 2 * kv_width)
    projected = jnp.dot(normed, full_qkv[:, :query_width], preferred_element_type=jnp.float32)
    kv_group, projected, out_left, out_right, other_first, sent_second = lax.optimization_barrier(
        (kv_group, projected, out_left, out_right, other_first, w_down[0, first_rows:])
    )
    other_second = lax.ppermute(sent_second, ALL, pairs)
    context = attention(
        projected, cosines, sines, kv_group, placing[None, :], prompt_start[:, None], my_place[:, None]
    )
    attn_out = jnp.concatenate(
        [
            jnp.dot(context, part, preferred_element_type=jnp.float32)
            for part in (out_left, out_right)
        ],
        axis=1,
    )
    attended = (hidden_in.astype(jnp.float32) + attn_out).astype(jnp.bfloat16)
    moe_in = rms_scaled(attended, moe_gain)

    outgoing = jnp.dot(pick, moe_in, preferred_element_type=jnp.float32).astype(jnp.bfloat16)
    outgoing, other_second = lax.optimization_barrier((outgoing, other_second))
    mine = lax.all_to_all(
        outgoing.reshape(CHIP_COUNT, MOST, model_width), CHIPS, 0, 0, tiled=True
    ).reshape(CHIP_COUNT * MOST, model_width)
    mates = lax.ppermute(mine, "core", CORES)
    weights = (w_gate_up[0], other_up, w_down[0], other_first, other_second)
    kept = keep.astype(jnp.int32).reshape(1)
    tiles = mine.shape[0] // ROW_TILE
    own_part = expert_half(kept, mine, weights, 0, tiles // 2)
    mates, own_part = lax.optimization_barrier((mates, own_part))
    for_mate = expert_half(kept, mates, weights, 0, tiles)
    from_mate = lax.ppermute(for_mate, "core", CORES)
    own_part = expert_half(kept, mine, weights, tiles // 2, tiles // 2, own_part)
    expert_out = (own_part.astype(jnp.float32) + from_mate.astype(jnp.float32)).astype(jnp.bfloat16)
    returned = lax.all_to_all(
        expert_out.reshape(CHIP_COUNT, MOST, model_width), CHIPS, 0, 0, tiled=True
    ).reshape(CHIP_COUNT * MOST, model_width)
    blended = jnp.dot(blend, returned, preferred_element_type=jnp.float32)
    mixture = blended[:row_count] + blended[row_count:]
    finished = (attended.astype(jnp.float32) + mixture).astype(jnp.bfloat16)

    home_rows = lax.all_to_all(
        finished.reshape(cache_size, deal_rows, model_width), CACHE, 0, 0, tiled=True
    ).reshape(row_count, model_width)
    my_base = group_base + my_index * row_count
    sender_place = lax.dynamic_slice_in_dim(
        placing.reshape(cache_size, row_count), my_index * deal_rows, deal_rows, axis=1
    ).reshape(-1)
    to_row = (sender_place[None, :] - my_base == row_ids[:, None]).astype(jnp.bfloat16)
    mixed = jnp.dot(to_row, home_rows, preferred_element_type=jnp.float32).astype(jnp.bfloat16)
    from_group = (placing[None, :] - my_base == row_ids[:, None]).astype(jnp.bfloat16)
    cached = jnp.dot(from_group, kv_group, preferred_element_type=jnp.float32).astype(jnp.bfloat16)
    return (mixed, cached[:, :kv_width], cached[:, kv_width:])


def solution(mesh):
    fine = Mesh(np.asarray(mesh.devices).reshape(tuple(SIZES[a] for a in ALL)), ALL)
    in_specs = (
        P(ALL, None),
        P(DP),
        P(ALL),
        P(),
        P(ALL, None),
        P(ALL, None),
        P(),
        P(ALL, None),
        P(ALL, None),
        P(ALL, None, None),
        P(ALL, None, None),
    )
    out_specs = (P(ALL, None), P(ALL, None), P(ALL, None))
    return jax.shard_map(
        per_device, mesh=fine, in_specs=in_specs, out_specs=out_specs, check_vma=False
    )
```

```python
import jax
import jax.numpy as jnp
import numpy as np
from jax import lax
from jax.experimental import pallas as pl
from jax.experimental.pallas import tpu as pltpu
from jax.sharding import Mesh
from jax.sharding import PartitionSpec as P

HD = 128
QH = 10
KVH = 2
TOP = 6
MOST = 16

DP = ("yh", "z", "core")
CACHE = ("yl", "x")
SIZES = {"yh": 2, "z": 4, "core": 2, "yl": 2, "x": 4}
ALL = DP + CACHE
CHIPS = ("yh", "z", "yl", "x")
CHIP_COUNT = 64

norm_eps = 1e-05
rope_base = 500000.0
masked_score = -1e30


def linear(yh, z, core, yl, x):
    return (((yh * 4 + z) * 2 + core) * 2 + yl) * 4 + x


def swap_pairs():
    pairs = []
    for yh in range(2):
        for z in range(4):
            for yl in range(2):
                for x in range(0, 4, 2):
                    low = linear(yh, z, 1, yl, x)
                    high = linear(yh, z, 0, yl, x + 1)
                    pairs += [(low, high), (high, low)]
    return pairs


def rms_scaled(features, gain_vector):
    widened = features.astype(jnp.float32)
    factor = lax.rsqrt(jnp.mean(widened * widened, axis=-1, keepdims=True) + norm_eps)
    return (widened * factor * gain_vector).astype(jnp.bfloat16)


def turned(head, cosines, sines):
    return (head * cosines + pltpu.roll(head, HD // 2, 1) * sines).astype(jnp.bfloat16)


def keys_values_kernel(projected, cosines, sines, out):
    for k in range(2 * KVH):
        columns = slice(k * HD, (k + 1) * HD)
        if k < KVH:
            part = turned(projected[:, columns], cosines[...], sines[...])
        else:
            part = projected[:, columns].astype(jnp.bfloat16)
        for device in range(out.shape[0]):
            out[device, :, columns] = part


def keys_values(projected, cosines, sines, copies):
    return pl.pallas_call(
        keys_values_kernel,
        out_shape=jax.ShapeDtypeStruct((copies,) + projected.shape, jnp.bfloat16),
    )(projected, cosines, sines)


def attention_kernel(projected, cosines, sines, kv_group, placing, start, place, out):
    allowed = (placing[...] >= start[...]) & (placing[...] <= place[...])
    share = QH // KVH
    for h in range(QH):
        columns = slice(h * HD, (h + 1) * HD)
        k = h // share
        query = turned(projected[:, columns], cosines[...], sines[...])
        scores = lax.dot_general(
            query,
            kv_group[:, k * HD : (k + 1) * HD],
            (((1,), (1,)), ((), ())),
            preferred_element_type=jnp.float32,
        ) * (HD ** (-0.5))
        scores = jnp.where(allowed, scores, masked_score)
        highest = jnp.max(scores, axis=1, keepdims=True)
        weights = jnp.where(allowed, jnp.exp(scores - highest), 0.0)
        denominator = jnp.sum(weights, axis=1, keepdims=True)
        numerator = jnp.dot(
            weights.astype(jnp.bfloat16),
            kv_group[:, (KVH + k) * HD : (KVH + k + 1) * HD],
            preferred_element_type=jnp.float32,
        )
        out[:, columns] = (numerator / denominator).astype(jnp.bfloat16)


def attention(projected, *operands):
    return pl.pallas_call(
        attention_kernel,
        out_shape=jax.ShapeDtypeStruct(projected.shape, jnp.bfloat16),
        compiler_params=pltpu.CompilerParams(vmem_limit_bytes=32 << 20),
    )(projected, *operands)


def spread(shard, axes, count):
    return lax.all_to_all(
        jnp.broadcast_to(shard[None], (count,) + shard.shape), axes, 0, 0, tiled=True
    )


CORES = [(0, 1), (1, 0)]
ROW_TILE = 256
UP_CHUNK = 640


def expert_kernel(keep, rows, own_up, other_up, own_down, other_first, other_second, *rest):
    out, up, down, up_sems, down_sems = rest[-5:]
    up_chunks = up.shape[0] // UP_CHUNK
    half_size = up.shape[1] // 2

    def up_copy(i, mine):
        part = pl.ds(i * UP_CHUNK, UP_CHUNK)
        source = own_up if mine else other_up
        return pltpu.make_async_copy(source.at[part], up.at[part], up_sems.at[i])

    down_half = down.shape[0] // 2

    def down_copy(i, mine):
        part = pl.ds(i * down_half, down_half)
        source = own_down.at[part] if mine else (other_first, other_second)[i]
        return pltpu.make_async_copy(source, down.at[part], down_sems.at[i])

    def finish(joined, wait):
        gate = joined[:, :half_size]
        active = (gate / (1.0 + jnp.exp(-gate)) * joined[:, half_size:]).astype(jnp.bfloat16)
        if wait:
            for i in range(2):
                down_copy(i, True).wait()
        out[...] = jnp.dot(active, down[...], preferred_element_type=jnp.float32).astype(jnp.bfloat16)

    @pl.when(pl.program_id(0) == 0)
    def _():
        @pl.when(keep[0] == 1)
        def _():
            for i in range(up_chunks):
                up_copy(i, True).start()
            for i in range(2):
                down_copy(i, True).start()

        @pl.when(keep[0] == 0)
        def _():
            for i in range(up_chunks):
                up_copy(i, False).start()
            for i in range(2):
                down_copy(i, False).start()

        joined = jnp.zeros((rows.shape[0], up.shape[1]), jnp.float32)
        for i in range(up_chunks):
            up_copy(i, True).wait()
            part = slice(i * UP_CHUNK, (i + 1) * UP_CHUNK)
            joined = joined + jnp.dot(
                rows[:, part], up[part, :], preferred_element_type=jnp.float32
            )
        finish(joined, True)

    @pl.when(pl.program_id(0) != 0)
    def _():
        finish(jnp.dot(rows[...], up[...], preferred_element_type=jnp.float32), False)


def expert_half(keep, rows, weights, first, tiles, filled=None):
    own_up, _, own_down, _, _ = weights
    anywhere = pl.BlockSpec(memory_space=pltpu.HBM)
    tile = pl.BlockSpec((ROW_TILE, rows.shape[1]), lambda i, keep: (first + i, 0))
    extra = [] if filled is None else [filled]
    return pl.pallas_call(
        expert_kernel,
        out_shape=jax.ShapeDtypeStruct(rows.shape, jnp.bfloat16),
        grid_spec=pltpu.PrefetchScalarGridSpec(
            num_scalar_prefetch=1,
            grid=(tiles,),
            in_specs=[tile] + [anywhere] * 5 + [pl.BlockSpec(memory_space=pl.ANY)] * len(extra),
            out_specs=tile,
            scratch_shapes=[
                pltpu.VMEM(own_up.shape, jnp.bfloat16),
                pltpu.VMEM(own_down.shape, jnp.bfloat16),
                pltpu.SemaphoreType.DMA((own_up.shape[0] // UP_CHUNK,)),
                pltpu.SemaphoreType.DMA((2,)),
            ],
        ),
        input_output_aliases={} if filled is None else {7: 0},
        compiler_params=pltpu.CompilerParams(
            dimension_semantics=("arbitrary",), vmem_limit_bytes=54 << 20
        ),
        cost_estimate=pl.CostEstimate(
            flops=2 * tiles * ROW_TILE * (own_up.size + own_down.size),
            transcendentals=tiles * ROW_TILE * own_down.shape[0],
            bytes_accessed=2 * (own_up.size + own_down.size)
            + 4 * tiles * ROW_TILE * rows.shape[1],
        ),
    )(keep, rows, *weights, *extra)


def per_device(
    hidden_in,
    placing,
    prompt_start,
    attn_gain,
    w_qkv,
    w_out,
    moe_gain,
    routes,
    route_weight,
    w_gate_up,
    w_down,
):
    row_count, model_width = hidden_in.shape
    query_width = QH * HD
    kv_width = KVH * HD
    my_index = lax.axis_index(CACHE)
    group_rows = placing.shape[0]
    cache_size = group_rows // row_count
    deal_rows = row_count // cache_size
    group_base = lax.axis_index(DP) * group_rows

    half_out = w_out.shape[1] // 2
    joint = jnp.concatenate(
        [w_qkv, jnp.concatenate([w_out[:, :half_out], w_out[:, half_out:]], axis=0)], axis=1
    )
    joint = spread(joint, CACHE, cache_size)
    qkv_rows = joint[:, :, : w_qkv.shape[1]].reshape(-1, w_qkv.shape[1])
    halves = joint[:, :, w_qkv.shape[1] :].reshape(cache_size, 2, w_out.shape[0], half_out)
    out_rows = jnp.concatenate([halves[:, 0], halves[:, 1]], axis=2).reshape(-1, w_out.shape[1])

    pairs = swap_pairs()
    down_half = w_down.shape[1] // 2
    sent_up, sent_first, qkv_rows, out_rows = lax.optimization_barrier(
        (w_gate_up[0], w_down[0, :down_half], qkv_rows, out_rows)
    )
    other_up = lax.ppermute(sent_up, ALL, pairs)
    other_first = lax.ppermute(sent_first, ALL, pairs)
    keep = lax.axis_index("x") % 2 == lax.axis_index("core")

    full_qkv = lax.all_gather(qkv_rows, DP, axis=0, tiled=True)
    full_out = lax.all_gather(out_rows, DP, axis=0, tiled=True)
    full_qkv, other_up = lax.optimization_barrier((full_qkv, other_up))

    my_place = lax.dynamic_slice_in_dim(placing, my_index * row_count, row_count)
    position = my_place - prompt_start

    bits = routes
    chip_of = (
        (bits & 0b111000)
        | ((bits & 0b000011) << 1)
        | ((bits & 0b000100) >> 2)
    )
    named = chip_of[:, :, None] == jnp.arange(CHIP_COUNT, dtype=jnp.int32)[None, None, :]
    member = jnp.any(named, axis=1)
    weight_of = jnp.sum(jnp.where(named, route_weight[:, :, None], 0.0), axis=1)
    row_ids = jnp.arange(row_count, dtype=jnp.int32)
    before = (row_ids[:, None] > row_ids[None, :]).astype(jnp.bfloat16)
    rank = jnp.dot(before, member.astype(jnp.bfloat16), preferred_element_type=jnp.float32)
    rank = jnp.where(member, rank.astype(jnp.int32), -1).T
    chosen = rank[:, None, :] == jnp.arange(MOST, dtype=jnp.int32)[None, :, None]
    chosen = chosen.reshape(CHIP_COUNT * MOST, row_count)
    pick = chosen.astype(jnp.bfloat16)
    weighted = jnp.where(
        chosen.reshape(CHIP_COUNT, MOST, row_count), weight_of.T[:, None, :], 0.0
    ).reshape(CHIP_COUNT * MOST, row_count)
    weighted_hi = lax.reduce_precision(weighted, 8, 7)
    weighted_lo = (weighted - weighted_hi).astype(jnp.bfloat16)
    blend = jnp.concatenate([weighted_hi.astype(jnp.bfloat16), weighted_lo], axis=1)

    normed = rms_scaled(hidden_in, attn_gain)
    half_size = HD // 2
    inverse = rope_base ** (-(jnp.arange(half_size, dtype=jnp.float32) * 2.0 / HD))
    angles = position.astype(jnp.float32)[:, None] * inverse[None, :]
    cosine = jnp.cos(angles)
    sine_part = jnp.sin(angles)
    cosines = jnp.concatenate([cosine, cosine], axis=1)
    sines = jnp.concatenate([-sine_part, sine_part], axis=1)
    kv_projected = jnp.dot(normed, full_qkv[:, query_width:], preferred_element_type=jnp.float32)
    kv_copies = keys_values(kv_projected, cosines, sines, cache_size)
    kv_group = lax.all_to_all(kv_copies, CACHE, 0, 0, tiled=True).reshape(group_rows, 2 * kv_width)
    projected = jnp.dot(normed, full_qkv[:, :query_width], preferred_element_type=jnp.float32)
    kv_group, projected, other_first, sent_second = lax.optimization_barrier(
        (kv_group, projected, other_first, w_down[0, down_half:])
    )
    other_second = lax.ppermute(sent_second, ALL, pairs)
    context = attention(
        projected, cosines, sines, kv_group, placing[None, :], prompt_start[:, None], my_place[:, None]
    )
    attn_out = jnp.dot(context, full_out, preferred_element_type=jnp.float32)
    attended = (hidden_in.astype(jnp.float32) + attn_out).astype(jnp.bfloat16)
    moe_in = rms_scaled(attended, moe_gain)

    outgoing = jnp.dot(pick, moe_in, preferred_element_type=jnp.float32).astype(jnp.bfloat16)
    outgoing, other_second = lax.optimization_barrier((outgoing, other_second))
    mine = lax.all_to_all(
        outgoing.reshape(CHIP_COUNT, MOST, model_width), CHIPS, 0, 0, tiled=True
    ).reshape(CHIP_COUNT * MOST, model_width)
    mates = lax.ppermute(mine, "core", CORES)
    weights = (w_gate_up[0], other_up, w_down[0], other_first, other_second)
    kept = keep.astype(jnp.int32).reshape(1)
    tiles = mine.shape[0] // ROW_TILE
    own_part = expert_half(kept, mine, weights, 0, tiles // 2)
    mates, own_part = lax.optimization_barrier((mates, own_part))
    for_mate = expert_half(kept, mates, weights, 0, tiles)
    from_mate = lax.ppermute(for_mate, "core", CORES)
    own_part = expert_half(kept, mine, weights, tiles // 2, tiles // 2, own_part)
    expert_out = (own_part.astype(jnp.float32) + from_mate.astype(jnp.float32)).astype(jnp.bfloat16)
    returned = lax.all_to_all(
        expert_out.reshape(CHIP_COUNT, MOST, model_width), CHIPS, 0, 0, tiled=True
    ).reshape(CHIP_COUNT * MOST, model_width)
    blended = lax.dot_general(
        blend, returned, (((0,), (0,)), ((), ())), preferred_element_type=jnp.float32
    )
    mixture = blended[:row_count] + blended[row_count:]
    finished = (attended.astype(jnp.float32) + mixture).astype(jnp.bfloat16)

    home_rows = lax.all_to_all(
        finished.reshape(cache_size, deal_rows, model_width), CACHE, 0, 0, tiled=True
    ).reshape(row_count, model_width)
    my_base = group_base + my_index * row_count
    sender_place = lax.dynamic_slice_in_dim(
        placing.reshape(cache_size, row_count), my_index * deal_rows, deal_rows, axis=1
    ).reshape(-1)
    to_row = (sender_place[None, :] - my_base == row_ids[:, None]).astype(jnp.bfloat16)
    mixed = jnp.dot(to_row, home_rows, preferred_element_type=jnp.float32).astype(jnp.bfloat16)
    from_group = (placing[None, :] - my_base == row_ids[:, None]).astype(jnp.bfloat16)
    cached = jnp.dot(from_group, kv_group, preferred_element_type=jnp.float32).astype(jnp.bfloat16)
    return (mixed, cached[:, :kv_width], cached[:, kv_width:])


def solution(mesh):
    fine = Mesh(np.asarray(mesh.devices).reshape(tuple(SIZES[a] for a in ALL)), ALL)
    in_specs = (
        P(ALL, None),
        P(DP),
        P(ALL),
        P(),
        P(ALL, None),
        P(ALL, None),
        P(),
        P(ALL, None),
        P(ALL, None),
        P(ALL, None, None),
        P(ALL, None, None),
    )
    out_specs = (P(ALL, None), P(ALL, None), P(ALL, None))
    return jax.shard_map(
        per_device, mesh=fine, in_specs=in_specs, out_specs=out_specs, check_vma=False
    )
```
